32 devices in a mesh: heads: 4 (over y, x), seq: 8 (over z, core).
Axes of the slice: x: 2, y: 2, z: 4, core: 2. Of those that a mesh axis runs over, the one named last changes fastest.
Arguments:
- queries: bfloat16 [6144, 2048], P('seq', 'heads'), may hold values from -6 to 6
- key_vectors: bfloat16 [6144, 2048], P('seq', 'heads'), may hold values from -10 to 10
- value_vectors: bfloat16 [6144, 2048], P('seq', 'heads'), may hold values from -6 to 6
- random_blocks: int32 [16, 96, 3], P('heads', 'seq'), may hold values from 0 to 95, as said below
- global_blocks: int32 [2], replicated, may hold values from 0 to 95, as said below
- out_weight: bfloat16 [2048, 4096], P('heads'), may hold values from -0.1875 to 0.1875
Outputs:
- layer_out: bfloat16 [6144, 4096], P('seq', 'heads')
The draws below stay inside these ranges and needn't reach their ends.
Inputs may be any that keep to these rules, and one draw needn't show every extreme that they name: `random_blocks`: entries are block numbers. Of the entries with heads of one group of 4 and query blocks of one run of 12 blocks, at most 28 lie in any one run of key blocks s * 12 to (s + 1) * 12 - 1, and exactly 28 lie in one such run. Entries may repeat. `global_blocks`: Distinct; the last entry is the last block, 95.
All inputs are finite; a program needn't handle non-finite values.
Results may differ from the reference program's by a relative error of at most 0.0095.
Values may be sent and summed in bfloat16 or wider, within the bound.
A program may use at most 128 MiB of HBM per device.

```python
import jax
import jax.numpy as jnp
from jax import lax

D = 4096
HEADS = 16
DH = 128
BLOCK = 64
RANDOM = 3
GLOBAL = 2
HEAD_GROUPS = 4
SHARDS = 8
HEADS_DEV = 4
BLOCKS_DEV = 12
BLOCKS_ALL = 96
TOKENS = 6144
REQUESTS = 144
CAPACITY = 28
N_HEADS = 4


def global_pick(key):
    ordering = jax.random.permutation(jax.random.fold_in(key, 7), BLOCKS_ALL - 1)
    chosen = ordering[:GLOBAL - 1].astype(jnp.int32)
    last_block = jnp.full((1,), BLOCKS_ALL - 1, jnp.int32)
    return jnp.concatenate([chosen, last_block]).astype(jnp.int32)


def draw_global_blocks(key, part):
    return global_pick(key)


def draw_queries(key, part):
    drawn = jnp.clip(jax.random.normal(jax.random.fold_in(key, 21), (TOKENS, HEADS * DH), jnp.float32), -6.0, 6.0)
    return drawn.astype(jnp.bfloat16)


def draw_key_vectors(key, part):
    drawn = jax.random.normal(jax.random.fold_in(key, 22), (TOKENS, HEADS * DH), jnp.float32)
    drawn = jnp.clip(2.0 * drawn, -10.0, 10.0)
    return drawn.astype(jnp.bfloat16)


def device_lists(key):
    tickets = jnp.arange(SHARDS * CAPACITY, dtype=jnp.int32) // CAPACITY
    busiest = jax.random.randint(jax.random.fold_in(key, 1), (), 0, SHARDS).astype(jnp.int32)
    shuffled = jax.random.permutation(jax.random.fold_in(key, 2), SHARDS * CAPACITY).astype(jnp.int32)
    ranking = shuffled - jnp.where(tickets == busiest, SHARDS * CAPACITY, 0).astype(jnp.int32)
    ordering = jnp.argsort(ranking)
    owners = tickets[ordering[:REQUESTS]]
    owners = owners[jax.random.permutation(jax.random.fold_in(key, 3), REQUESTS)]
    local_ids = jax.random.randint(jax.random.fold_in(key, 4), (REQUESTS,), 0, BLOCKS_DEV).astype(jnp.int32)
    return (owners * BLOCKS_DEV + local_ids).reshape(HEADS_DEV, BLOCKS_DEV, RANDOM)


def draw_random_blocks(key, part):
    devices = HEAD_GROUPS * SHARDS
    device_keys = jax.vmap(lambda number: jax.random.fold_in(key, number))(jnp.arange(devices))
    tables = jax.vmap(device_lists)(device_keys)
    tables = tables.reshape(HEAD_GROUPS, SHARDS, HEADS_DEV, BLOCKS_DEV, RANDOM).transpose(0, 2, 1, 3, 4)
    return tables.reshape(HEADS, BLOCKS_ALL, RANDOM).astype(jnp.int32)


def with_spikes(values, stream_key, source, target, blocks, factor):
    owner, partner = [(jnp.arange(values.shape[dim]) // (values.shape[dim] // blocks)).reshape([-1 if axis == dim else 1 for axis in range(values.ndim)]) for dim in (source, target)]
    chosen = jax.random.permutation(stream_key, blocks)[partner]
    strong = (owner == chosen) | (owner == (partner + blocks // 2) % blocks)
    return jnp.where(strong, factor * values, values)


def level_of(own_key, dims, split, smallest, high):
    level = 1.0
    for axis_at, parts in split:
        steps = jax.random.uniform(jax.random.fold_in(jax.random.fold_in(own_key, 6), axis_at), (parts,), jnp.float32, smallest / len(split), high / len(split))
        level = level * jnp.repeat(jnp.exp(steps), dims[axis_at] // parts).reshape((-1,) + (1,) * (len(dims) - 1 - axis_at))
    return level


def scatter_about(stream_key, dims, deviation, bound, shards=(), kind=jnp.bfloat16):
    loudness = level_of(stream_key, dims, shards, -0.22, 0.18) if shards else 1.0
    values = jax.random.normal(stream_key, dims, jnp.float32) * deviation * loudness
    return jnp.minimum(jnp.maximum(values, -bound), bound).astype(kind)


def noise_with(own_key, extent, deviation, limit, cuts, heavy, kind=jnp.bfloat16):
    values = deviation * jax.random.normal(own_key, extent, jnp.float32)
    if cuts:
        values = values * level_of(own_key, extent, cuts, -0.22, 0.18)
    return jnp.clip(with_spikes(values, jax.random.fold_in(own_key, 3), *heavy), -limit, limit).astype(kind)


def setup_inputs(seed: int = 0) -> dict:
    splits = jax.random.split(jax.random.key(seed), 7)
    return {
        "queries": draw_queries(jax.random.fold_in(splits[6], 71), 0),
        "key_vectors": draw_key_vectors(jax.random.fold_in(splits[6], 71), 0),
        "value_vectors": scatter_about(splits[2], (TOKENS, HEADS * DH), 1.0, 6.0, ((0, 8), (1, 4))),
        "random_blocks": draw_random_blocks(jax.random.fold_in(splits[6], 71), 0),
        "global_blocks": draw_global_blocks(jax.random.fold_in(splits[6], 71), 0),
        "out_weight": noise_with(splits[5], (HEADS * DH, D), (HEADS * DH) ** -0.5, 0.1875, ((0, 4),), (0, 1, 4, 2.0)),
    }


def head_attention(operands, global_blocks):
    q_head, k_head, v_head, rand_head = operands
    block_count = q_head.shape[0] // BLOCK
    score_multiplier = DH ** -0.5
    query_block_tiles = q_head.reshape(block_count, BLOCK, DH)
    k_tiles = k_head.reshape(block_count, BLOCK, DH)
    v_tiles = v_head.reshape(block_count, BLOCK, DH)

    def gather_keys(tiles):
        zero_tile = jnp.zeros((1, BLOCK, DH), tiles.dtype)
        padded = jnp.concatenate([zero_tile, tiles, zero_tile], axis=0)
        window = jnp.stack([padded[:-2], padded[1:-1], padded[2:]], axis=1)
        random_part = tiles[rand_head]
        global_part = jnp.broadcast_to(tiles[global_blocks][None], (block_count, GLOBAL, BLOCK, DH))
        joined = jnp.concatenate([window, random_part, global_part], axis=1)
        return joined.reshape(block_count, -1, DH)

    window_key_rows = gather_keys(k_tiles)
    window_value_rows = gather_keys(v_tiles)
    logit_scores = jnp.einsum("hmo,hzo->hmz", query_block_tiles.astype(jnp.float32), window_key_rows.astype(jnp.float32)) * score_multiplier
    column_block = jnp.arange(window_key_rows.shape[1]) // BLOCK
    row_block = jnp.arange(block_count)
    valid_keys = jnp.where(column_block[None, :] == 0, row_block[:, None] > 0,
                           jnp.where(column_block[None, :] == 2, row_block[:, None] < block_count - 1, True))
    logit_scores = jnp.where(valid_keys[:, None, :], logit_scores, -jnp.inf)
    row_peak = jnp.max(logit_scores, axis=-1, keepdims=True)
    exponent = jnp.exp(logit_scores - row_peak)
    softmax_divisor = jnp.sum(exponent, axis=-1, keepdims=True)
    rounded_scores = lax.optimization_barrier(exponent.astype(jnp.bfloat16))
    sparse_result = jnp.einsum("afg,agv->afv", rounded_scores.astype(jnp.float32), window_value_rows.astype(jnp.float32)) / softmax_divisor
    sparse_result = sparse_result.astype(jnp.bfloat16)
    global_query = query_block_tiles[global_blocks].reshape(GLOBAL * BLOCK, DH)
    global_scores = jnp.dot(global_query, k_head.T, preferred_element_type=jnp.float32) * score_multiplier
    global_top = jnp.max(global_scores, axis=-1, keepdims=True)
    global_exp = jnp.exp(global_scores - global_top)
    global_out = jnp.dot(global_exp, v_head.astype(jnp.float32), precision=lax.Precision.HIGHEST)
    global_out = global_out / jnp.sum(global_exp, axis=-1, keepdims=True)
    global_out = global_out.astype(jnp.bfloat16).reshape(GLOBAL, BLOCK, DH)
    return sparse_result.at[global_blocks].set(global_out)


def reference(queries, key_vectors, value_vectors, random_blocks, global_blocks, out_weight):
    tokens_all = queries.shape[0]

    def split_heads(matrix):
        return matrix.reshape(tokens_all, HEADS, DH).transpose(1, 0, 2)

    attended = lax.map(lambda operands: head_attention(operands, global_blocks),
                       (split_heads(queries), split_heads(key_vectors), split_heads(value_vectors), random_blocks))
    merged = attended.reshape(HEADS, tokens_all, DH).transpose(1, 0, 2).reshape(tokens_all, HEADS * DH)
    group_width = HEADS_DEV * DH
    result = jnp.zeros((tokens_all, D), jnp.float32)
    for group_index in range(N_HEADS):
        start = group_index * group_width
        partial_sum = jnp.dot(merged[:, start:start + group_width], out_weight[start:start + group_width],
                              preferred_element_type=jnp.float32)
        rounded_scores = lax.optimization_barrier(partial_sum.astype(jnp.bfloat16))
        result = result + rounded_scores.astype(jnp.float32)
    return result.astype(jnp.bfloat16)
```

```python
import functools

import jax
import jax.numpy as jnp
from jax import lax
from jax.experimental import pallas as pl
from jax.experimental.pallas import tpu as pltpu
from jax.sharding import PartitionSpec as P

DH = 128
BLOCK = 64
RANDOM = 3
GLOBAL = 2


def extended(shard, sides, width):
    for axis, dim in sides:
        peers, length = (lax.axis_size(axis), shard.shape[dim])
        up = [(i, (i + 1) % peers) for i in range(peers - 1)]
        down = [(j, i) for i, j in up]
        last = lax.slice_in_dim(shard, length - width, length, axis=dim)
        leading = lax.slice_in_dim(shard, 0, width, axis=dim)
        before = lax.ppermute(last, axis, up)
        after = lax.ppermute(leading, axis, down)
        shard = jnp.concatenate([before, shard, after], axis=dim)
    return shard


def joined(shard, axis, combine):
    everything = jax.tree.map(
        lambda part, kind: lax.all_gather(part.astype(kind), axis),
        shard,
        (jnp.bfloat16, jnp.bfloat16, jnp.bfloat16),
    )

    def take(k):
        return jax.tree.map(lambda part, own: part[k].astype(own.dtype), everything, shard)

    return lax.fori_loop(
        1, lax.axis_size(axis), lambda k, so_far: combine(so_far, take(k)), take(0)
    )


def combine_parts(first, second):
    top_first, total_first, out_first = first
    top_second, total_second, out_second = second
    highest = jnp.maximum(top_first, top_second)
    scale_first = jnp.exp(top_first - highest)
    scale_second = jnp.exp(top_second - highest)
    return (
        highest,
        total_first * scale_first + total_second * scale_second,
        out_first * scale_first[..., None] + out_second * scale_second[..., None],
    )


def rows_at(table, index):
    chosen = (index[:, None] == jnp.arange(table.shape[0], dtype=jnp.int32)[None, :]).astype(table.dtype)
    return jnp.dot(chosen, table, preferred_element_type=jnp.float32).astype(table.dtype)


def blocks_at(tiles, index):
    return jnp.stack([lax.dynamic_index_in_dim(tiles, index[r], 1, False) for r in range(GLOBAL)], axis=1)


def requested(queries, key_vectors, value_vectors, random_blocks, global_blocks, out_weight):
    shards = lax.axis_size("seq")
    my_index = lax.axis_index("seq")
    tok_rows, features = queries.shape
    heads_here = features // DH
    blocks_here = tok_rows // BLOCK
    requests = heads_here * blocks_here * RANDOM
    capacity = max(2, 3 * requests // (2 * shards) + 1)
    score_multiplier = DH ** (-0.5)
    query_block_tiles = queries.reshape(blocks_here, BLOCK, heads_here, DH).transpose(2, 0, 1, 3)
    stacked = jnp.concatenate([key_vectors, value_vectors], axis=1)
    padded = extended(stacked, (("seq", 0),), BLOCK)
    kv_tiles = padded.reshape(blocks_here + 2, BLOCK, 2, heads_here, DH).transpose(3, 0, 1, 2, 4)
    own_tiles = kv_tiles[:, 1:-1]
    table = own_tiles.reshape(heads_here * blocks_here, BLOCK * 2 * DH)
    flat_lists = random_blocks.reshape(requests)
    head_of = jnp.arange(requests, dtype=jnp.int32) // (blocks_here * RANDOM)
    code_flat = head_of * blocks_here + flat_lists % blocks_here
    holders = flat_lists // blocks_here
    order = jnp.arange(requests, dtype=jnp.int32)
    earlier = (order[None, :] < order[:, None]) & (holders[None, :] == holders[:, None])
    slot_flat = holders * capacity + jnp.sum(earlier.astype(jnp.int32), axis=1)
    slots = jnp.arange(shards * capacity, dtype=jnp.int32)
    asked = jnp.sum(
        jnp.where(slots[:, None] == slot_flat[None, :], code_flat[None, :], 0), axis=1
    ).reshape(shards, capacity)
    answered = lax.all_to_all(asked, "seq", split_axis=0, concat_axis=0, tiled=True)
    arrived = lax.all_to_all(
        rows_at(table, answered.reshape(shards * capacity)),
        "seq",
        split_axis=0,
        concat_axis=0,
        tiled=True,
    )
    fetched = rows_at(arrived, slot_flat)
    fetched = fetched.reshape(heads_here, blocks_here, RANDOM, BLOCK, 2, DH)
    holder_glob = global_blocks // blocks_here
    place_glob = global_blocks % blocks_here
    mine_glob = holder_glob == my_index
    global_q_local = blocks_at(query_block_tiles, place_glob)
    global_kv_local = blocks_at(own_tiles, place_glob)
    owned_mask = mine_glob.astype(jnp.float32)
    summed_query, summed_pairs = lax.psum(
        (
            global_q_local.astype(jnp.float32) * owned_mask[None, :, None, None],
            global_kv_local.astype(jnp.float32) * owned_mask[None, :, None, None, None],
        ),
        "seq",
    )
    global_query = summed_query.astype(jnp.bfloat16)
    global_pairs = summed_pairs.astype(jnp.bfloat16)
    window = jnp.stack([kv_tiles[:, :-2], kv_tiles[:, 1:-1], kv_tiles[:, 2:]], axis=2)
    spread_global = jnp.broadcast_to(
        global_pairs[:, None], (heads_here, blocks_here, GLOBAL, BLOCK, 2, DH)
    )
    listed = jnp.concatenate([window, fetched, spread_global], axis=2).reshape(
        heads_here, blocks_here, -1, 2, DH
    )
    window_key_rows = listed[:, :, :, 0]
    window_value_rows = listed[:, :, :, 1]
    logit_scores = (
        jnp.einsum(
            "hbqd,hbkd->hbqk",
            query_block_tiles,
            window_key_rows,
            preferred_element_type=jnp.float32,
        )
        * score_multiplier
    )
    column_block = jnp.arange(window_key_rows.shape[2]) // BLOCK
    row_global = my_index * blocks_here + jnp.arange(blocks_here)
    valid_keys = jnp.where(
        column_block[None, :] == 0,
        row_global[:, None] > 0,
        jnp.where(column_block[None, :] == 2, row_global[:, None] < shards * blocks_here - 1, True),
    )
    logit_scores = jnp.where(valid_keys[None, :, None, :], logit_scores, -jnp.inf)
    row_peak = jnp.max(logit_scores, axis=-1, keepdims=True)
    exponent = jnp.exp(logit_scores - row_peak)
    softmax_divisor = jnp.sum(exponent, axis=-1, keepdims=True)
    sparse_result = (
        jnp.einsum(
            "hbqk,hbkd->hbqd",
            exponent.astype(jnp.bfloat16),
            window_value_rows,
            preferred_element_type=jnp.float32,
        )
        / softmax_divisor
    )
    sparse_result = sparse_result.astype(jnp.bfloat16)
    local_keys = own_tiles[:, :, :, 0].reshape(heads_here, tok_rows, DH)
    local_values = own_tiles[:, :, :, 1].reshape(heads_here, tok_rows, DH).astype(jnp.float32)
    global_rows_q = global_query.reshape(heads_here, GLOBAL * BLOCK, DH)
    global_scores = (
        jnp.einsum("hqd,hkd->hqk", global_rows_q, local_keys, preferred_element_type=jnp.float32)
        * score_multiplier
    )
    local_top = jnp.max(global_scores, axis=-1)
    global_exp = jnp.exp(global_scores - local_top[..., None])
    top_all, total_all, out_all = joined(
        (
            local_top,
            jnp.sum(global_exp, axis=-1),
            jnp.einsum("hqk,hkd->hqd", global_exp, local_values, precision=lax.Precision.HIGHEST),
        ),
        "seq",
        combine_parts,
    )
    global_out = (
        (out_all / total_all[..., None]).astype(jnp.bfloat16).reshape(heads_here, GLOBAL, BLOCK, DH)
    )
    block_ids = jnp.arange(blocks_here)
    for glob_index in range(GLOBAL):
        replace_mask = mine_glob[glob_index] & (block_ids == place_glob[glob_index])
        sparse_result = jnp.where(
            replace_mask[None, :, None, None], global_out[:, glob_index][:, None], sparse_result
        )
    attention = sparse_result.transpose(1, 2, 0, 3).reshape(tok_rows, features)
    partial_out = jnp.dot(attention, out_weight, preferred_element_type=jnp.float32)
    return lax.psum_scatter(
        partial_out.astype(jnp.bfloat16), "heads", scatter_dimension=1, tiled=True
    )


MESH = pl.DeviceIdType.MESH
ANY = pl.BlockSpec(memory_space=pl.ANY)
VMEM_BYTES = 56 * 1024 * 1024
SIDE = 2
CORES = 2
TILE = 256


def peers(shards, groups, me, group):
    line = [{"seq": lax.rem(me + k, shards)} for k in range(1, shards)]
    return line + [{"heads": lax.rem(group + k, groups)} for k in range(1, groups)]


def remote(src, dst, send, recv, device):
    return pltpu.make_async_remote_copy(
        src_ref=src,
        dst_ref=dst,
        send_sem=send,
        recv_sem=recv,
        device_id=device,
        device_id_type=MESH,
    )


def crossed(a, b, shards):
    total, bit = 0, 1
    while bit < shards:
        if isinstance(b, int):
            here, there = lax.rem(lax.div(a, bit), 2), (b // bit) % 2
        else:
            here, there = lax.rem(lax.div(a, bit), 2), lax.rem(lax.div(b, bit), 2)
        total = total + bit * (here + there - 2 * here * there)
        bit *= 2
    return total


def layer_kernel(
    shards, heads, groups,
    q_ref, k_ref, v_ref, list_ref, glob_ref, w_ref, out_ref,
    q_here, named, named_near, chosen, glob_all, glob_q, q_all, k_all, v_all, list_all, list_here,
    w_here, glob_here, glob_peak, glob_total, o_here, att, acc,
    send_sem, recv_sem, pass_send, pass_recv, w_send, w_recv, own_sem, glob_send, glob_recv,
    o_send, o_recv, side_send, side_recv, half_send, half_recv,
):
    me = lax.axis_index("seq")
    group = lax.axis_index("heads")
    rows, width = out_ref.shape
    depth = w_ref.shape[0]
    share = CORES
    piece = rows // share
    blocks = rows // BLOCK
    local = blocks // share
    last = shards * blocks - 1
    scale = DH ** (-0.5)
    nt = (((1,), (1,)), ((), ()))
    my_head = lax.div(me, share)
    my_part = lax.rem(me, share)
    partner = my_head * share + (1 - my_part)
    pairs = ((k_ref, k_all), (v_ref, v_all))
    count = len(pairs)

    barrier = pltpu.get_barrier_semaphore()
    known = peers(shards, groups, me, group)
    for device in known:
        pl.semaphore_signal(barrier, inc=1, device_id=device, device_id_type=MESH)

    def window(src, head, part):
        return src.at[
            pl.ds(part * local, local), :, pl.ds(pl.multiple_of(head * DH, DH), DH)
        ]

    def landing(dst, source, part):
        return dst.at[pl.ds(source * blocks + part * local, local)]

    load_q = pltpu.make_async_copy(q_ref, q_here, own_sem.at[0])
    load_q.start()
    own_kv = [
        pltpu.make_async_copy(
            window(src, my_head, my_part), landing(dst, me, my_part), own_sem.at[1 + t]
        )
        for t, (src, dst) in enumerate(pairs)
    ]
    own_q = pltpu.make_async_copy(
        window(q_ref, my_head, my_part), q_all.at[me], own_sem.at[3]
    )
    own_list = pltpu.make_async_copy(list_ref, list_all.at[me], own_sem.at[4])
    own_w = pltpu.make_async_copy(
        w_ref.at[:, pl.ds(pl.multiple_of(group * width, width), width)],
        w_here.at[group],
        own_sem.at[5],
    )
    for copy in (*own_kv, own_q, own_list, own_w):
        copy.start()
    load_q.wait()
    for r in range(GLOBAL):
        picked = q_here[lax.rem(glob_ref[r], blocks)]
        for head in range(heads):
            named[r, head] = picked[:, head * DH : (head + 1) * DH]
    pl.semaphore_wait(barrier, len(known))

    swap = remote(
        named.at[1 - my_part], named_near, glob_send.at[0], glob_recv.at[0], {"seq": partner}
    )
    swap.start()
    sends = {}
    for x in range(1, shards):
        sends[x, count] = remote(
            list_ref,
            list_all.at[me],
            send_sem.at[x, count],
            recv_sem.at[x, count],
            {"seq": crossed(me, x, shards)},
        )
        sends[x, count].start()

    def offer(x):
        to = crossed(me, x, shards)
        head, part = lax.div(to, share), lax.rem(to, share)
        for t, (src, dst) in enumerate(pairs):
            sends[x, t] = remote(
                window(src, head, part),
                landing(dst, me, part),
                send_sem.at[x, t],
                recv_sem.at[x, t],
                {"seq": to},
            )
            sends[x, t].start()

    for x in (2, shards // 2):
        offer(x)
    swap.wait_recv()
    wanted = lax.div(glob_ref[my_part], blocks)
    for head in range(heads):
        apart = jnp.full((BLOCK, DH), wanted, jnp.int32) - jnp.full((BLOCK, DH), partner, jnp.int32)
        chosen[head] = jnp.where(apart == 0, named_near[head], named[my_part, head])
    own_glob = pltpu.make_async_copy(chosen.at[my_head], glob_all.at[my_head], own_sem.at[0])
    own_glob.start()
    globs = {}
    for n in range(1, heads):
        to = crossed(me, n * share, shards)
        globs[n] = remote(
            chosen.at[lax.div(to, share)],
            glob_all.at[my_head],
            glob_send.at[n],
            glob_recv.at[n],
            {"seq": to},
        )
        globs[n].start()
    for x in range(1, shards):
        if x not in (2, shards // 2):
            offer(x)

    def weight_rows(of, part):
        slab = depth // share
        return w_here.at[of, pl.ds(pl.multiple_of(part * slab, slab), slab), :]

    weights = {}
    for k in range(1, groups):
        to = lax.rem(group + k, groups)
        slab = depth // share
        weights[k] = remote(
            w_ref.at[
                pl.ds(pl.multiple_of(my_part * slab, slab), slab),
                pl.ds(pl.multiple_of(to * width, width), width),
            ],
            weight_rows(group, my_part),
            w_send.at[0, k],
            w_recv.at[0, k],
            {"heads": to},
        )
        weights[k].start()

    for x in range(1, shards):
        to = crossed(me, x, shards)
        sends[x, count + 1] = remote(
            window(q_ref, lax.div(to, share), lax.rem(to, share)),
            q_all.at[me],
            send_sem.at[x, count + 1],
            recv_sem.at[x, count + 1],
            {"seq": to},
        )
        sends[x, count + 1].start()

    own_list.wait()
    for x in range(1, shards):
        sends[x, count].wait_recv()
    told = pltpu.make_async_copy(list_all, list_here, own_sem.at[4])
    told.start()
    own_glob.wait()
    for n in range(1, heads):
        globs[n].wait_recv()
    glob_q[my_part] = glob_all[lax.div(wanted, share)]
    glob_pass = remote(
        glob_q.at[my_part], glob_q.at[my_part], glob_send.at[heads], glob_recv.at[heads], {"seq": partner}
    )
    glob_pass.start()
    told.wait()
    glob_pass.wait_recv()

    def offered(x, t):
        src, dst = pairs[t]
        return remote(
            window(src, 0, 0),
            landing(dst, me, my_part),
            send_sem.at[x, t],
            recv_sem.at[x, t],
            {"seq": crossed(me, x, shards)},
        )

    def handed(x, t):
        region = landing(pairs[t][1], crossed(me, x, shards), my_part)
        return remote(region, region, pass_send.at[x, t], pass_recv.at[x, t], {"seq": partner})

    size = GLOBAL * BLOCK
    glob_peak[...] = jnp.full((size, 1), -jnp.inf, jnp.float32)
    glob_total[...] = jnp.zeros((size, 1), jnp.float32)
    glob_here[...] = jnp.zeros((size, DH), jnp.float32)

    def step(c):
        at = pl.ds(c * blocks, blocks)
        scores = lax.dot_general(
            glob_q[...].reshape(size, DH),
            k_all[at].reshape(rows, DH),
            nt,
            preferred_element_type=jnp.float32,
        ) * scale
        peak = glob_peak[...]
        top = jnp.maximum(peak, jnp.max(scores, axis=-1, keepdims=True))
        fade = jnp.exp(peak - top)
        heavy = jnp.exp(scores - top)
        glob_peak[...] = top
        glob_total[...] = glob_total[...] * fade + jnp.sum(heavy, axis=-1, keepdims=True)
        glob_here[...] = glob_here[...] * fade + jnp.dot(
            heavy.astype(jnp.bfloat16),
            v_all[at].reshape(rows, DH),
            preferred_element_type=jnp.float32,
        )

    @pl.loop(0, heads + 1)
    def _(m):
        @pl.when(m < heads)
        def _():
            for p in range(share):
                x = m * share + p
                for t in range(count):
                    if p == 0:
                        @pl.when(m == 0)
                        def _(t=t):
                            own_kv[t].wait()

                        @pl.when(m > 0)
                        def _(x=x, t=t):
                            offered(x, t).wait_recv()
                    else:
                        offered(x, t).wait_recv()
                    handed(x, t).start()

        @pl.when(m > 0)
        def _():
            for p in range(share):
                for t in range(count):
                    handed((m - 1) * share + p, t).wait_recv()
            chip = crossed(my_head, m - 1, heads)
            for p in range(share):
                step(chip * share + p)

    glob_here[...] = glob_here[...] / glob_total[...]
    for k in range(1, groups):
        weights[k].wait_recv()
        of = lax.rem(group + groups - k, groups)
        weights[k, 1] = remote(
            weight_rows(of, my_part),
            weight_rows(of, my_part),
            w_send.at[1, k],
            w_recv.at[1, k],
            {"seq": partner},
        )
        weights[k, 1].start()
    own_q.wait()

    lanes = (3 + RANDOM + GLOBAL) * BLOCK
    column = lax.broadcasted_iota(jnp.int32, (1, lanes), 1) // BLOCK

    def one(i, s, j):
        here = my_part * local + j
        b = s * blocks + here
        listed = [jnp.maximum(b - 1, 0), b, jnp.minimum(b + 1, last)]
        for r in range(RANDOM):
            listed.append(list_here[s, r, my_head, here])
        for r in range(GLOBAL):
            listed.append(glob_ref[r])
        keys = jnp.concatenate([k_all[x] for x in listed], axis=0)
        values = jnp.concatenate([v_all[x] for x in listed], axis=0)
        scores = lax.dot_general(
            q_all[s, j], keys, nt, preferred_element_type=jnp.float32
        ) * scale
        hidden = ((column == 0) & (b == 0)) | ((column == 2) & (b == last))
        scores = jnp.where(hidden, -jnp.inf, scores)
        peak = jnp.max(scores, axis=-1, keepdims=True)
        heavy = jnp.exp(scores - peak)
        total = jnp.sum(heavy, axis=-1, keepdims=True)
        mixed = jnp.dot(heavy.astype(jnp.bfloat16), values, preferred_element_type=jnp.float32)
        result = mixed / total
        for r in range(GLOBAL):
            apart = jnp.full((BLOCK, DH), b, jnp.int32) - jnp.full((BLOCK, DH), glob_ref[r], jnp.int32)
            result = jnp.where(apart == 0, glob_here[r * BLOCK : (r + 1) * BLOCK, :], result)
        o_here[i, j * BLOCK : (j + 1) * BLOCK, :] = result.astype(jnp.bfloat16)

    across = lax.div(group, SIDE)
    along = lax.rem(group, SIDE)
    sides = (across * SIDE + (1 - along), (1 - across) * SIDE + along)
    diagonal = (1 - across) * SIDE + (1 - along)

    def spot(of, source):
        part = lax.rem(source, share)
        return att.at[
            of,
            pl.ds(pl.multiple_of(part * piece, piece), piece),
            pl.ds(pl.multiple_of(lax.div(source, share) * DH, DH), DH),
        ]

    def asked(i):
        return remote(
            window(q_ref, 0, 0),
            q_all.at[me],
            send_sem.at[i, count + 1],
            recv_sem.at[i, count + 1],
            {"seq": crossed(me, i, shards)},
        )

    def kept():
        return pltpu.make_async_copy(o_here.at[0], spot(group, me), own_sem.at[0])

    def back(i):
        return remote(
            o_here.at[i],
            spot(group, me),
            o_send.at[i],
            o_recv.at[i],
            {"seq": crossed(me, i, shards)},
        )

    def sideways(i, n):
        region = spot(group, crossed(me, i, shards))
        return remote(
            region, region, side_send.at[n, i], side_recv.at[n, i], {"heads": sides[n]}
        )

    def corner(i, n):
        half = piece // 2
        region = spot(sides[n], crossed(me, i, shards)).at[n * half : (n + 1) * half, :]
        return remote(
            region, region, half_send.at[n, i], half_recv.at[n, i], {"heads": sides[1 - n]}
        )

    def spread(i):
        if not isinstance(i, int):
            back(i).wait_recv()
        elif i == 0:
            kept().wait()
        else:
            back(i).wait_recv()
        for n in range(SIDE):
            sideways(i, n).start()

    def turn(i):
        for n in range(SIDE):
            sideways(i, n).wait_recv()
            corner(i, n).start()

    def arrive(i):
        for n in range(SIDE):
            corner(i, n).wait_recv()

    @pl.loop(0, shards)
    def _(i):
        s = crossed(me, i, shards)

        @pl.when(i > 0)
        def _():
            asked(i).wait_recv()

        for j in range(local):
            one(i, s, j)

        @pl.when(i == 0)
        def _():
            kept().start()

        @pl.when(i > 0)
        def _():
            back(i).start()

        for n in range(share):
            @pl.when(i == n + 1)
            def _(n=n):
                spread(n)

            @pl.when(i == n + share + 2)
            def _(n=n):
                turn(n)

    half_depth = depth // 2
    my_side = lax.div(my_head, heads // 2)

    def project(parts, near, slices, first=False, final=False):
        base = (my_side if near else 1 - my_side) * half_depth
        deep = pl.ds(pl.multiple_of(base, half_depth), half_depth)

        for part in slices:
            at = pl.ds(pl.multiple_of(part * piece, piece), piece)

            @pl.loop(0, width // TILE)
            def _(c):
                cols = pl.ds(pl.multiple_of(c * TILE, TILE), TILE)
                term = sum(
                    jnp.dot(
                        att[of, at, deep],
                        w_here[of, deep, cols],
                        preferred_element_type=jnp.float32,
                    )
                    for of in parts
                )
                if not first:
                    term = term + acc[at, cols]
                if final:
                    out_ref[at, cols] = term.astype(out_ref.dtype)
                else:
                    acc[at, cols] = term

    both = (my_part, 1 - my_part)
    near_end = shards // 2
    for i in range(share, near_end + 1):
        spread(i)
        if i > share:
            turn(i - 1)
    own_w.wait()
    for k in range(1, groups):
        weights[k, 1].wait_recv()
    project((group,), True, both, first=True)
    spread(near_end + 1)
    turn(near_end)
    for i in range(near_end):
        arrive(i)
    project((*sides, diagonal), True, both)
    for i in range(near_end + 2, shards):
        spread(i)
        turn(i - 1)
    project((group,), False, both)
    turn(shards - 1)
    project(sides, False, both)
    for i in range(near_end, shards - 1):
        arrive(i)
    project((diagonal,), False, both[:1], final=True)
    arrive(shards - 1)
    project((diagonal,), False, both[1:], final=True)

    swap.wait_send()
    glob_pass.wait_send()
    for copy in (*sends.values(), *globs.values(), *weights.values()):
        copy.wait_send()

    @pl.loop(0, shards)
    def _(i):
        for t in range(count):
            handed(i, t).wait_send()

        @pl.when(i > 0)
        def _():
            back(i).wait_send()

        for n in range(SIDE):
            sideways(i, n).wait_send()
            corner(i, n).wait_send()


def regrouped(queries, key_vectors, value_vectors, random_blocks, global_blocks, out_weight):
    shards = lax.axis_size("seq")
    groups = lax.axis_size("heads")
    rows, features = queries.shape
    heads = features // DH
    blocks = rows // BLOCK
    piece = rows // CORES
    depth, model = out_weight.shape
    width = model // groups
    lists = random_blocks.transpose(2, 0, 1)
    dma = pltpu.SemaphoreType.DMA
    bf16 = jnp.bfloat16
    whole = pltpu.VMEM((shards * blocks, BLOCK, DH), bf16)
    split = (blocks, BLOCK, features)
    return pl.pallas_call(
        functools.partial(layer_kernel, shards, heads, groups),
        out_shape=pltpu.VMEM((rows, width), bf16),
        in_specs=[ANY] * 4 + [pl.BlockSpec(memory_space=pltpu.SMEM), ANY],
        out_specs=pl.BlockSpec(memory_space=pltpu.VMEM),
        scratch_shapes=[
            pltpu.VMEM(split, bf16),
            pltpu.VMEM((GLOBAL, heads, BLOCK, DH), bf16),
            pltpu.VMEM((heads, BLOCK, DH), bf16),
            pltpu.VMEM((heads, BLOCK, DH), bf16),
            pltpu.VMEM((heads, BLOCK, DH), bf16),
            pltpu.VMEM((GLOBAL, BLOCK, DH), bf16),
            pltpu.VMEM((shards, blocks // CORES, BLOCK, DH), bf16),
            whole,
            whole,
            pltpu.VMEM((shards, *lists.shape), jnp.int32),
            pltpu.SMEM((shards, *lists.shape), jnp.int32),
            pltpu.VMEM((groups, depth, width), bf16),
            pltpu.VMEM((GLOBAL * BLOCK, DH), jnp.float32),
            pltpu.VMEM((GLOBAL * BLOCK, 1), jnp.float32),
            pltpu.VMEM((GLOBAL * BLOCK, 1), jnp.float32),
            pltpu.VMEM((shards, piece, DH), bf16),
            pltpu.VMEM((groups, rows, features), bf16),
            pltpu.VMEM((rows, width), jnp.float32),
            dma((shards, 4)),
            dma((shards, 4)),
            dma((shards, 2)),
            dma((shards, 2)),
            dma((2, groups)),
            dma((2, groups)),
            dma((6,)),
            dma((heads + 1,)),
            dma((heads + 1,)),
            dma((shards,)),
            dma((shards,)),
            dma((SIDE, shards)),
            dma((SIDE, shards)),
            dma((SIDE, shards)),
            dma((SIDE, shards)),
        ],
        compiler_params=pltpu.CompilerParams(
            collective_id=0, has_side_effects=True, vmem_limit_bytes=VMEM_BYTES
        ),
        name="layer",
    )(
        queries.reshape(split),
        key_vectors.reshape(split),
        value_vectors.reshape(split),
        lists,
        global_blocks,
        out_weight,
    )


def on_device(queries, key_vectors, value_vectors, random_blocks, global_blocks, out_weight):
    shards = lax.axis_size("seq")
    groups = lax.axis_size("heads")
    rows, features = queries.shape
    heads = features // DH
    fits = shards == heads * CORES and heads == 4 and groups == SIDE * SIDE and GLOBAL == CORES
    body = regrouped if fits and (rows // BLOCK) % CORES == 0 else requested
    return body(queries, key_vectors, value_vectors, random_blocks, global_blocks, out_weight)


def solution(mesh):
    placed = (
        P("seq", "heads"),
        P("seq", "heads"),
        P("seq", "heads"),
        P("heads", "seq", None),
        P(),
        P("heads", None),
    )
    return jax.shard_map(
        on_device, mesh=mesh, in_specs=placed, out_specs=P("seq", "heads"), check_vma=False
    )
```

```python
import functools

import jax
import jax.numpy as jnp
from jax import lax
from jax.experimental import pallas as pl
from jax.experimental.pallas import tpu as pltpu
from jax.sharding import PartitionSpec as P

DH = 128
BLOCK = 64
RANDOM = 3
GLOBAL = 2


def extended(shard, sides, width):
    for axis, dim in sides:
        peers, length = (lax.axis_size(axis), shard.shape[dim])
        up = [(i, (i + 1) % peers) for i in range(peers - 1)]
        down = [(j, i) for i, j in up]
        last = lax.slice_in_dim(shard, length - width, length, axis=dim)
        leading = lax.slice_in_dim(shard, 0, width, axis=dim)
        before = lax.ppermute(last, axis, up)
        after = lax.ppermute(leading, axis, down)
        shard = jnp.concatenate([before, shard, after], axis=dim)
    return shard


def joined(shard, axis, combine):
    everything = jax.tree.map(
        lambda part, kind: lax.all_gather(part.astype(kind), axis),
        shard,
        (jnp.bfloat16, jnp.bfloat16, jnp.bfloat16),
    )

    def take(k):
        return jax.tree.map(lambda part, own: part[k].astype(own.dtype), everything, shard)

    return lax.fori_loop(
        1, lax.axis_size(axis), lambda k, so_far: combine(so_far, take(k)), take(0)
    )


def combine_parts(first, second):
    top_first, total_first, out_first = first
    top_second, total_second, out_second = second
    highest = jnp.maximum(top_first, top_second)
    scale_first = jnp.exp(top_first - highest)
    scale_second = jnp.exp(top_second - highest)
    return (
        highest,
        total_first * scale_first + total_second * scale_second,
        out_first * scale_first[..., None] + out_second * scale_second[..., None],
    )


def rows_at(table, index):
    chosen = (index[:, None] == jnp.arange(table.shape[0], dtype=jnp.int32)[None, :]).astype(table.dtype)
    return jnp.dot(chosen, table, preferred_element_type=jnp.float32).astype(table.dtype)


def blocks_at(tiles, index):
    return jnp.stack([lax.dynamic_index_in_dim(tiles, index[r], 1, False) for r in range(GLOBAL)], axis=1)


def requested(queries, key_vectors, value_vectors, random_blocks, global_blocks, out_weight):
    shards = lax.axis_size("seq")
    my_index = lax.axis_index("seq")
    tok_rows, features = queries.shape
    heads_here = features // DH
    blocks_here = tok_rows // BLOCK
    requests = heads_here * blocks_here * RANDOM
    capacity = max(2, 3 * requests // (2 * shards) + 1)
    score_multiplier = DH ** (-0.5)
    query_block_tiles = queries.reshape(blocks_here, BLOCK, heads_here, DH).transpose(2, 0, 1, 3)
    stacked = jnp.concatenate([key_vectors, value_vectors], axis=1)
    padded = extended(stacked, (("seq", 0),), BLOCK)
    kv_tiles = padded.reshape(blocks_here + 2, BLOCK, 2, heads_here, DH).transpose(3, 0, 1, 2, 4)
    own_tiles = kv_tiles[:, 1:-1]
    table = own_tiles.reshape(heads_here * blocks_here, BLOCK * 2 * DH)
    flat_lists = random_blocks.reshape(requests)
    head_of = jnp.arange(requests, dtype=jnp.int32) // (blocks_here * RANDOM)
    code_flat = head_of * blocks_here + flat_lists % blocks_here
    holders = flat_lists // blocks_here
    order = jnp.arange(requests, dtype=jnp.int32)
    earlier = (order[None, :] < order[:, None]) & (holders[None, :] == holders[:, None])
    slot_flat = holders * capacity + jnp.sum(earlier.astype(jnp.int32), axis=1)
    slots = jnp.arange(shards * capacity, dtype=jnp.int32)
    asked = jnp.sum(
        jnp.where(slots[:, None] == slot_flat[None, :], code_flat[None, :], 0), axis=1
    ).reshape(shards, capacity)
    answered = lax.all_to_all(asked, "seq", split_axis=0, concat_axis=0, tiled=True)
    arrived = lax.all_to_all(
        rows_at(table, answered.reshape(shards * capacity)),
        "seq",
        split_axis=0,
        concat_axis=0,
        tiled=True,
    )
    fetched = rows_at(arrived, slot_flat)
    fetched = fetched.reshape(heads_here, blocks_here, RANDOM, BLOCK, 2, DH)
    holder_glob = global_blocks // blocks_here
    place_glob = global_blocks % blocks_here
    mine_glob = holder_glob == my_index
    global_q_local = blocks_at(query_block_tiles, place_glob)
    global_kv_local = blocks_at(own_tiles, place_glob)
    owned_mask = mine_glob.astype(jnp.float32)
    summed_query, summed_pairs = lax.psum(
        (
            global_q_local.astype(jnp.float32) * owned_mask[None, :, None, None],
            global_kv_local.astype(jnp.float32) * owned_mask[None, :, None, None, None],
        ),
        "seq",
    )
    global_query = summed_query.astype(jnp.bfloat16)
    global_pairs = summed_pairs.astype(jnp.bfloat16)
    window = jnp.stack([kv_tiles[:, :-2], kv_tiles[:, 1:-1], kv_tiles[:, 2:]], axis=2)
    spread_global = jnp.broadcast_to(
        global_pairs[:, None], (heads_here, blocks_here, GLOBAL, BLOCK, 2, DH)
    )
    listed = jnp.concatenate([window, fetched, spread_global], axis=2).reshape(
        heads_here, blocks_here, -1, 2, DH
    )
    window_key_rows = listed[:, :, :, 0]
    window_value_rows = listed[:, :, :, 1]
    logit_scores = (
        jnp.einsum(
            "hbqd,hbkd->hbqk",
            query_block_tiles,
            window_key_rows,
            preferred_element_type=jnp.float32,
        )
        * score_multiplier
    )
    column_block = jnp.arange(window_key_rows.shape[2]) // BLOCK
    row_global = my_index * blocks_here + jnp.arange(blocks_here)
    valid_keys = jnp.where(
        column_block[None, :] == 0,
        row_global[:, None] > 0,
        jnp.where(column_block[None, :] == 2, row_global[:, None] < shards * blocks_here - 1, True),
    )
    logit_scores = jnp.where(valid_keys[None, :, None, :], logit_scores, -jnp.inf)
    row_peak = jnp.max(logit_scores, axis=-1, keepdims=True)
    exponent = jnp.exp(logit_scores - row_peak)
    softmax_divisor = jnp.sum(exponent, axis=-1, keepdims=True)
    sparse_result = (
        jnp.einsum(
            "hbqk,hbkd->hbqd",
            exponent.astype(jnp.bfloat16),
            window_value_rows,
            preferred_element_type=jnp.float32,
        )
        / softmax_divisor
    )
    sparse_result = sparse_result.astype(jnp.bfloat16)
    local_keys = own_tiles[:, :, :, 0].reshape(heads_here, tok_rows, DH)
    local_values = own_tiles[:, :, :, 1].reshape(heads_here, tok_rows, DH).astype(jnp.float32)
    global_rows_q = global_query.reshape(heads_here, GLOBAL * BLOCK, DH)
    global_scores = (
        jnp.einsum("hqd,hkd->hqk", global_rows_q, local_keys, preferred_element_type=jnp.float32)
        * score_multiplier
    )
    local_top = jnp.max(global_scores, axis=-1)
    global_exp = jnp.exp(global_scores - local_top[..., None])
    top_all, total_all, out_all = joined(
        (
            local_top,
            jnp.sum(global_exp, axis=-1),
            jnp.einsum("hqk,hkd->hqd", global_exp, local_values, precision=lax.Precision.HIGHEST),
        ),
        "seq",
        combine_parts,
    )
    global_out = (
        (out_all / total_all[..., None]).astype(jnp.bfloat16).reshape(heads_here, GLOBAL, BLOCK, DH)
    )
    block_ids = jnp.arange(blocks_here)
    for glob_index in range(GLOBAL):
        replace_mask = mine_glob[glob_index] & (block_ids == place_glob[glob_index])
        sparse_result = jnp.where(
            replace_mask[None, :, None, None], global_out[:, glob_index][:, None], sparse_result
        )
    attention = sparse_result.transpose(1, 2, 0, 3).reshape(tok_rows, features)
    partial_out = jnp.dot(attention, out_weight, preferred_element_type=jnp.float32)
    return lax.psum_scatter(
        partial_out.astype(jnp.bfloat16), "heads", scatter_dimension=1, tiled=True
    )


MESH = pl.DeviceIdType.MESH
ANY = pl.BlockSpec(memory_space=pl.ANY)
VMEM_BYTES = 56 * 1024 * 1024
SIDE = 2
CORES = 2
TILE = 256


PLAN = ((3, (0,), ()), (4, (1,), ()), (5, (2,), (0,)), (6, (3,), (1,)), (7, (), (2, 3)))


def peers(shards, groups, me, group):
    line = [{"seq": lax.rem(me + k, shards)} for k in range(1, shards)]
    return line + [{"heads": lax.rem(group + k, groups)} for k in range(1, groups)]


def remote(src, dst, send, recv, device):
    return pltpu.make_async_remote_copy(
        src_ref=src,
        dst_ref=dst,
        send_sem=send,
        recv_sem=recv,
        device_id=device,
        device_id_type=MESH,
    )


def crossed(a, b, shards):
    total, bit = 0, 1
    while bit < shards:
        if isinstance(b, int):
            here, there = lax.rem(lax.div(a, bit), 2), (b // bit) % 2
        else:
            here, there = lax.rem(lax.div(a, bit), 2), lax.rem(lax.div(b, bit), 2)
        total = total + bit * (here + there - 2 * here * there)
        bit *= 2
    return total


def layer_kernel(
    shards, heads, groups,
    q_ref, k_ref, v_ref, list_ref, glob_ref, w_ref, out_ref,
    q_here, named, named_near, chosen, glob_all, glob_q, q_all, k_all, v_all, list_all, list_here,
    w_here, glob_here, glob_peak, glob_total, o_here, att, acc,
    send_sem, recv_sem, pass_send, pass_recv, w_send, w_recv, own_sem, glob_send, glob_recv,
    o_send, o_recv, side_send, side_recv, half_send, half_recv,
):
    me = lax.axis_index("seq")
    group = lax.axis_index("heads")
    rows, width = out_ref.shape
    depth = w_ref.shape[0]
    share = CORES
    piece = rows // share
    blocks = rows // BLOCK
    local = blocks // share
    last = shards * blocks - 1
    scale = DH ** (-0.5)
    nt = (((1,), (1,)), ((), ()))
    my_head = lax.div(me, share)
    my_part = lax.rem(me, share)
    partner = my_head * share + (1 - my_part)
    pairs = ((k_ref, k_all), (v_ref, v_all))
    count = len(pairs)

    barrier = pltpu.get_barrier_semaphore()
    known = peers(shards, groups, me, group)
    for device in known:
        pl.semaphore_signal(barrier, inc=1, device_id=device, device_id_type=MESH)

    def window(src, head, part):
        return src.at[
            pl.ds(part * local, local), :, pl.ds(pl.multiple_of(head * DH, DH), DH)
        ]

    def landing(dst, source, part):
        return dst.at[pl.ds(source * blocks + part * local, local)]

    load_q = pltpu.make_async_copy(q_ref, q_here, own_sem.at[0])
    load_q.start()
    own_kv = [
        pltpu.make_async_copy(
            window(src, my_head, my_part), landing(dst, me, my_part), own_sem.at[1 + t]
        )
        for t, (src, dst) in enumerate(pairs)
    ]
    own_q = pltpu.make_async_copy(
        window(q_ref, my_head, my_part), q_all.at[me], own_sem.at[3]
    )
    own_list = pltpu.make_async_copy(list_ref, list_all.at[me], own_sem.at[4])
    own_w = pltpu.make_async_copy(
        w_ref.at[:, pl.ds(pl.multiple_of(group * width, width), width)],
        w_here.at[group],
        own_sem.at[5],
    )
    for copy in (*own_kv, own_q, own_list, own_w):
        copy.start()
    load_q.wait()
    for r in range(GLOBAL):
        picked = q_here[lax.rem(glob_ref[r], blocks)]
        for head in range(heads):
            named[r, head] = picked[:, head * DH : (head + 1) * DH]
    pl.semaphore_wait(barrier, len(known))

    swap = remote(
        named.at[1 - my_part], named_near, glob_send.at[0], glob_recv.at[0], {"seq": partner}
    )
    swap.start()
    sends = {}
    for x in range(1, shards):
        sends[x, count] = remote(
            list_ref,
            list_all.at[me],
            send_sem.at[x, count],
            recv_sem.at[x, count],
            {"seq": crossed(me, x, shards)},
        )
        sends[x, count].start()

    def offer(x):
        to = crossed(me, x, shards)
        head, part = lax.div(to, share), lax.rem(to, share)
        for t, (src, dst) in enumerate(pairs):
            sends[x, t] = remote(
                window(src, head, part),
                landing(dst, me, part),
                send_sem.at[x, t],
                recv_sem.at[x, t],
                {"seq": to},
            )
            sends[x, t].start()

    for x in (2, shards // 2):
        offer(x)
    swap.wait_recv()
    wanted = lax.div(glob_ref[my_part], blocks)
    for head in range(heads):
        apart = jnp.full((BLOCK, DH), wanted, jnp.int32) - jnp.full((BLOCK, DH), partner, jnp.int32)
        chosen[head] = jnp.where(apart == 0, named_near[head], named[my_part, head])
    own_glob = pltpu.make_async_copy(chosen.at[my_head], glob_all.at[my_head], own_sem.at[0])
    own_glob.start()
    globs = {}
    for n in range(1, heads):
        to = crossed(me, n * share, shards)
        globs[n] = remote(
            chosen.at[lax.div(to, share)],
            glob_all.at[my_head],
            glob_send.at[n],
            glob_recv.at[n],
            {"seq": to},
        )
        globs[n].start()
    for x in range(1, shards):
        if x not in (2, shards // 2):
            offer(x)

    def weight_rows(of, part):
        slab = depth // share
        return w_here.at[of, pl.ds(pl.multiple_of(part * slab, slab), slab), :]

    weights = {}
    for k in range(1, groups):
        to = lax.rem(group + k, groups)
        slab = depth // share
        weights[k] = remote(
            w_ref.at[
                pl.ds(pl.multiple_of(my_part * slab, slab), slab),
                pl.ds(pl.multiple_of(to * width, width), width),
            ],
            weight_rows(group, my_part),
            w_send.at[0, k],
            w_recv.at[0, k],
            {"heads": to},
        )
        weights[k].start()

    for x in range(1, shards):
        to = crossed(me, x, shards)
        sends[x, count + 1] = remote(
            window(q_ref, lax.div(to, share), lax.rem(to, share)),
            q_all.at[me],
            send_sem.at[x, count + 1],
            recv_sem.at[x, count + 1],
            {"seq": to},
        )
        if x < shards - 1:
            sends[x, count + 1].start()

    own_list.wait()
    for x in range(1, shards):
        sends[x, count].wait_recv()
    told = pltpu.make_async_copy(list_all, list_here, own_sem.at[4])
    told.start()
    own_glob.wait()
    for n in range(1, heads):
        globs[n].wait_recv()
    glob_q[my_part] = glob_all[lax.div(wanted, share)]
    glob_pass = remote(
        glob_q.at[my_part], glob_q.at[my_part], glob_send.at[heads], glob_recv.at[heads], {"seq": partner}
    )
    glob_pass.start()
    told.wait()
    glob_pass.wait_recv()

    def offered(x, t):
        src, dst = pairs[t]
        return remote(
            window(src, 0, 0),
            landing(dst, me, my_part),
            send_sem.at[x, t],
            recv_sem.at[x, t],
            {"seq": crossed(me, x, shards)},
        )

    def handed(x, t):
        region = landing(pairs[t][1], crossed(me, x, shards), my_part)
        return remote(region, region, pass_send.at[x, t], pass_recv.at[x, t], {"seq": partner})

    size = GLOBAL * BLOCK
    glob_peak[...] = jnp.full((size, 1), -jnp.inf, jnp.float32)
    glob_total[...] = jnp.zeros((size, 1), jnp.float32)
    glob_here[...] = jnp.zeros((size, DH), jnp.float32)

    def step(c):
        at = pl.ds(c * blocks, blocks)
        scores = lax.dot_general(
            glob_q[...].reshape(size, DH),
            k_all[at].reshape(rows, DH),
            nt,
            preferred_element_type=jnp.float32,
        ) * scale
        peak = glob_peak[...]
        top = jnp.maximum(peak, jnp.max(scores, axis=-1, keepdims=True))
        fade = jnp.exp(peak - top)
        heavy = jnp.exp(scores - top)
        glob_peak[...] = top
        glob_total[...] = glob_total[...] * fade + jnp.sum(heavy, axis=-1, keepdims=True)
        glob_here[...] = glob_here[...] * fade + jnp.dot(
            heavy.astype(jnp.bfloat16),
            v_all[at].reshape(rows, DH),
            preferred_element_type=jnp.float32,
        )

    @pl.loop(0, heads + 1)
    def _(m):
        @pl.when(m < heads)
        def _():
            for p in range(share):
                x = m * share + p
                for t in range(count):
                    if p == 0:
                        @pl.when(m == 0)
                        def _(t=t):
                            own_kv[t].wait()

                        @pl.when(m > 0)
                        def _(x=x, t=t):
                            offered(x, t).wait_recv()
                    else:
                        offered(x, t).wait_recv()
                    handed(x, t).start()

        @pl.when(m > 0)
        def _():
            for p in range(share):
                for t in range(count):
                    handed((m - 1) * share + p, t).wait_recv()
            chip = crossed(my_head, m - 1, heads)
            for p in range(share):
                step(chip * share + p)

    glob_here[...] = glob_here[...] / glob_total[...]
    for k in range(1, groups):
        weights[k].wait_recv()
        of = lax.rem(group + groups - k, groups)
        weights[k, 1] = remote(
            weight_rows(of, my_part),
            weight_rows(of, my_part),
            w_send.at[1, k],
            w_recv.at[1, k],
            {"seq": partner},
        )
        weights[k, 1].start()
    own_q.wait()

    lanes = (3 + RANDOM + GLOBAL) * BLOCK
    column = lax.broadcasted_iota(jnp.int32, (1, lanes), 1) // BLOCK

    def one(i, s, j):
        here = my_part * local + j
        b = s * blocks + here
        listed = [jnp.maximum(b - 1, 0), b, jnp.minimum(b + 1, last)]
        for r in range(RANDOM):
            listed.append(list_here[s, r, my_head, here])
        for r in range(GLOBAL):
            listed.append(glob_ref[r])
        keys = jnp.concatenate([k_all[x] for x in listed], axis=0)
        values = jnp.concatenate([v_all[x] for x in listed], axis=0)
        scores = lax.dot_general(
            q_all[s, j], keys, nt, preferred_element_type=jnp.float32
        ) * scale
        hidden = ((column == 0) & (b == 0)) | ((column == 2) & (b == last))
        scores = jnp.where(hidden, -jnp.inf, scores)
        peak = jnp.max(scores, axis=-1, keepdims=True)
        heavy = jnp.exp(scores - peak)
        total = jnp.sum(heavy, axis=-1, keepdims=True)
        mixed = jnp.dot(heavy.astype(jnp.bfloat16), values, preferred_element_type=jnp.float32)
        result = mixed / total
        for r in range(GLOBAL):
            apart = jnp.full((BLOCK, DH), b, jnp.int32) - jnp.full((BLOCK, DH), glob_ref[r], jnp.int32)
            result = jnp.where(apart == 0, glob_here[r * BLOCK : (r + 1) * BLOCK, :], result)
        o_here[i, j * BLOCK : (j + 1) * BLOCK, :] = result.astype(jnp.bfloat16)

    across = lax.div(group, SIDE)
    along = lax.rem(group, SIDE)
    sides = (across * SIDE + (1 - along), (1 - across) * SIDE + along)
    diagonal = (1 - across) * SIDE + (1 - along)

    def spot(of, source):
        part = lax.rem(source, share)
        return att.at[
            of,
            pl.ds(pl.multiple_of(part * piece, piece), piece),
            pl.ds(pl.multiple_of(lax.div(source, share) * DH, DH), DH),
        ]

    def asked(i):
        return remote(
            window(q_ref, 0, 0),
            q_all.at[me],
            send_sem.at[i, count + 1],
            recv_sem.at[i, count + 1],
            {"seq": crossed(me, i, shards)},
        )

    def kept():
        return pltpu.make_async_copy(o_here.at[0], spot(group, me), own_sem.at[0])

    def back(i):
        return remote(
            o_here.at[i],
            spot(group, me),
            o_send.at[i],
            o_recv.at[i],
            {"seq": crossed(me, i, shards)},
        )

    def sideways(i, n):
        region = spot(group, crossed(me, i, shards))
        return remote(
            region, region, side_send.at[n, i], side_recv.at[n, i], {"heads": sides[n]}
        )

    def corner(i, n):
        half = piece // 2
        region = spot(sides[n], crossed(me, i, shards)).at[n * half : (n + 1) * half, :]
        return remote(
            region, region, half_send.at[n, i], half_recv.at[n, i], {"heads": sides[1 - n]}
        )

    def spread(i):
        if not isinstance(i, int):
            back(i).wait_recv()
        elif i == 0:
            kept().wait()
        else:
            back(i).wait_recv()
        for n in range(SIDE):
            sideways(i, n).start()

    def turn(i):
        for n in range(SIDE):
            sideways(i, n).wait_recv()
            corner(i, n).start()

    def arrive(i):
        for n in range(SIDE):
            corner(i, n).wait_recv()

    @pl.loop(0, shards)
    def _(n):
        i = n + share * (1 - 2 * lax.rem(lax.div(n, share), 2)) * (1 - lax.div(n, 2 * share))
        s = crossed(me, i, shards)

        @pl.when(i > 0)
        def _():
            asked(i).wait_recv()

        for j in range(local):
            one(i, s, j)

        @pl.when(i == 0)
        def _():
            kept().start()

        @pl.when(i > 0)
        def _():
            back(i).start()

        @pl.when(n == 1)
        def _():
            far = crossed(me, shards - 1, shards)
            remote(
                window(q_ref, lax.div(far, share), lax.rem(far, share)),
                q_all.at[me],
                send_sem.at[shards - 1, count + 1],
                recv_sem.at[shards - 1, count + 1],
                {"seq": far},
            ).start()

        for when, spreads, turns in PLAN:
            @pl.when(n == when)
            def _(spreads=spreads, turns=turns):
                for at in spreads:
                    spread(at)
                for at in turns:
                    turn(at)

    half_depth = depth // 2
    my_side = lax.div(my_head, heads // 2)

    def project(parts, near, slices, first=False, final=False):
        base = (my_side if near else 1 - my_side) * half_depth
        deep = pl.ds(pl.multiple_of(base, half_depth), half_depth)

        for part in slices:
            at = pl.ds(pl.multiple_of(part * piece, piece), piece)

            @pl.loop(0, width // TILE)
            def _(c):
                cols = pl.ds(pl.multiple_of(c * TILE, TILE), TILE)
                term = sum(
                    jnp.dot(
                        att[of, at, deep],
                        w_here[of, deep, cols],
                        preferred_element_type=jnp.float32,
                    )
                    for of in parts
                )
                if not first:
                    term = term + acc[at, cols]
                if final:
                    out_ref[at, cols] = term.astype(out_ref.dtype)
                else:
                    acc[at, cols] = term

    def project_piece(i, parts, final=False):
        source = crossed(me, i, shards)
        at = pl.ds(pl.multiple_of(lax.rem(source, share) * piece, piece), piece)
        deep = pl.ds(pl.multiple_of(lax.div(source, share) * DH, DH), DH)

        @pl.loop(0, width // TILE)
        def _(c):
            cols = pl.ds(pl.multiple_of(c * TILE, TILE), TILE)
            term = acc[at, cols] + jnp.dot(
                jnp.concatenate([att[of, at, deep] for of in parts], axis=1),
                jnp.concatenate([w_here[of, deep, cols] for of in parts], axis=0),
                preferred_element_type=jnp.float32,
            )
            if final:
                out_ref[at, cols] = term.astype(out_ref.dtype)
            else:
                acc[at, cols] = term

    both = (my_part, 1 - my_part)
    ends = (group, diagonal)
    near_end = shards // 2
    own_w.wait()
    for k in range(1, groups):
        weights[k, 1].wait_recv()
    project((group,), True, both, first=True)
    spread(near_end)
    for i in range(near_end):
        arrive(i)
    project((*sides, diagonal), True, both)
    for i in range(near_end + 1, shards):
        spread(i)
        turn(i - 1)
        if i > near_end + 1:
            arrive(i - 2)
            project_piece(i - 2, sides)
            project_piece(i - 2, ends)
    turn(shards - 1)
    arrive(shards - 2)
    project_piece(shards - 2, sides)
    project_piece(shards - 2, ends, final=True)
    project_piece(shards - 1, sides)
    arrive(shards - 1)
    project_piece(shards - 1, ends, final=True)

    swap.wait_send()
    glob_pass.wait_send()
    for copy in (*sends.values(), *globs.values(), *weights.values()):
        copy.wait_send()

    @pl.loop(0, shards)
    def _(i):
        for t in range(count):
            handed(i, t).wait_send()

        @pl.when(i > 0)
        def _():
            back(i).wait_send()

        for n in range(SIDE):
            sideways(i, n).wait_send()
            corner(i, n).wait_send()


def regrouped(queries, key_vectors, value_vectors, random_blocks, global_blocks, out_weight):
    shards = lax.axis_size("seq")
    groups = lax.axis_size("heads")
    rows, features = queries.shape
    heads = features // DH
    blocks = rows // BLOCK
    piece = rows // CORES
    depth, model = out_weight.shape
    width = model // groups
    lists = random_blocks.transpose(2, 0, 1)
    dma = pltpu.SemaphoreType.DMA
    bf16 = jnp.bfloat16
    whole = pltpu.VMEM((shards * blocks, BLOCK, DH), bf16)
    split = (blocks, BLOCK, features)
    return pl.pallas_call(
        functools.partial(layer_kernel, shards, heads, groups),
        out_shape=pltpu.VMEM((rows, width), bf16),
        in_specs=[ANY] * 4 + [pl.BlockSpec(memory_space=pltpu.SMEM), ANY],
        out_specs=pl.BlockSpec(memory_space=pltpu.VMEM),
        scratch_shapes=[
            pltpu.VMEM(split, bf16),
            pltpu.VMEM((GLOBAL, heads, BLOCK, DH), bf16),
            pltpu.VMEM((heads, BLOCK, DH), bf16),
            pltpu.VMEM((heads, BLOCK, DH), bf16),
            pltpu.VMEM((heads, BLOCK, DH), bf16),
            pltpu.VMEM((GLOBAL, BLOCK, DH), bf16),
            pltpu.VMEM((shards, blocks // CORES, BLOCK, DH), bf16),
            whole,
            whole,
            pltpu.VMEM((shards, *lists.shape), jnp.int32),
            pltpu.SMEM((shards, *lists.shape), jnp.int32),
            pltpu.VMEM((groups, depth, width), bf16),
            pltpu.VMEM((GLOBAL * BLOCK, DH), jnp.float32),
            pltpu.VMEM((GLOBAL * BLOCK, 1), jnp.float32),
            pltpu.VMEM((GLOBAL * BLOCK, 1), jnp.float32),
            pltpu.VMEM((shards, piece, DH), bf16),
            pltpu.VMEM((groups, rows, features), bf16),
            pltpu.VMEM((rows, width), jnp.float32),
            dma((shards, 4)),
            dma((shards, 4)),
            dma((shards, 2)),
            dma((shards, 2)),
            dma((2, groups)),
            dma((2, groups)),
            dma((6,)),
            dma((heads + 1,)),
            dma((heads + 1,)),
            dma((shards,)),
            dma((shards,)),
            dma((SIDE, shards)),
            dma((SIDE, shards)),
            dma((SIDE, shards)),
            dma((SIDE, shards)),
        ],
        compiler_params=pltpu.CompilerParams(
            collective_id=0, has_side_effects=True, vmem_limit_bytes=VMEM_BYTES
        ),
        name="layer",
    )(
        queries.reshape(split),
        key_vectors.reshape(split),
        value_vectors.reshape(split),
        lists,
        global_blocks,
        out_weight,
    )


def on_device(queries, key_vectors, value_vectors, random_blocks, global_blocks, out_weight):
    shards = lax.axis_size("seq")
    groups = lax.axis_size("heads")
    rows, features = queries.shape
    heads = features // DH
    fits = shards == heads * CORES and heads == 4 and groups == SIDE * SIDE and GLOBAL == CORES
    body = regrouped if fits and (rows // BLOCK) % CORES == 0 else requested
    return body(queries, key_vectors, value_vectors, random_blocks, global_blocks, out_weight)


def solution(mesh):
    placed = (
        P("seq", "heads"),
        P("seq", "heads"),
        P("seq", "heads"),
        P("heads", "seq", None),
        P(),
        P("heads", None),
    )
    return jax.shard_map(
        on_device, mesh=mesh, in_specs=placed, out_specs=P("seq", "heads"), check_vma=False
    )
```

```python
import functools

import jax
import jax.numpy as jnp
from jax import lax
from jax.experimental import pallas as pl
from jax.experimental.pallas import tpu as pltpu
from jax.sharding import PartitionSpec as P

DH = 128
BLOCK = 64
RANDOM = 3
GLOBAL = 2


def extended(shard, sides, width):
    for axis, dim in sides:
        peers, length = (lax.axis_size(axis), shard.shape[dim])
        up = [(i, (i + 1) % peers) for i in range(peers - 1)]
        down = [(j, i) for i, j in up]
        last = lax.slice_in_dim(shard, length - width, length, axis=dim)
        leading = lax.slice_in_dim(shard, 0, width, axis=dim)
        before = lax.ppermute(last, axis, up)
        after = lax.ppermute(leading, axis, down)
        shard = jnp.concatenate([before, shard, after], axis=dim)
    return shard


def joined(shard, axis, combine):
    everything = jax.tree.map(
        lambda part, kind: lax.all_gather(part.astype(kind), axis),
        shard,
        (jnp.bfloat16, jnp.bfloat16, jnp.bfloat16),
    )

    def take(k):
        return jax.tree.map(lambda part, own: part[k].astype(own.dtype), everything, shard)

    return lax.fori_loop(
        1, lax.axis_size(axis), lambda k, so_far: combine(so_far, take(k)), take(0)
    )


def combine_parts(first, second):
    top_first, total_first, out_first = first
    top_second, total_second, out_second = second
    highest = jnp.maximum(top_first, top_second)
    scale_first = jnp.exp(top_first - highest)
    scale_second = jnp.exp(top_second - highest)
    return (
        highest,
        total_first * scale_first + total_second * scale_second,
        out_first * scale_first[..., None] + out_second * scale_second[..., None],
    )


def rows_at(table, index):
    chosen = (index[:, None] == jnp.arange(table.shape[0], dtype=jnp.int32)[None, :]).astype(table.dtype)
    return jnp.dot(chosen, table, preferred_element_type=jnp.float32).astype(table.dtype)


def blocks_at(tiles, index):
    return jnp.stack([lax.dynamic_index_in_dim(tiles, index[r], 1, False) for r in range(GLOBAL)], axis=1)


def requested(queries, key_vectors, value_vectors, random_blocks, global_blocks, out_weight):
    shards = lax.axis_size("seq")
    my_index = lax.axis_index("seq")
    tok_rows, features = queries.shape
    heads_here = features // DH
    blocks_here = tok_rows // BLOCK
    requests = heads_here * blocks_here * RANDOM
    capacity = max(2, 3 * requests // (2 * shards) + 1)
    score_multiplier = DH ** (-0.5)
    query_block_tiles = queries.reshape(blocks_here, BLOCK, heads_here, DH).transpose(2, 0, 1, 3)
    stacked = jnp.concatenate([key_vectors, value_vectors], axis=1)
    padded = extended(stacked, (("seq", 0),), BLOCK)
    kv_tiles = padded.reshape(blocks_here + 2, BLOCK, 2, heads_here, DH).transpose(3, 0, 1, 2, 4)
    own_tiles = kv_tiles[:, 1:-1]
    table = own_tiles.reshape(heads_here * blocks_here, BLOCK * 2 * DH)
    flat_lists = random_blocks.reshape(requests)
    head_of = jnp.arange(requests, dtype=jnp.int32) // (blocks_here * RANDOM)
    code_flat = head_of * blocks_here + flat_lists % blocks_here
    holders = flat_lists // blocks_here
    order = jnp.arange(requests, dtype=jnp.int32)
    earlier = (order[None, :] < order[:, None]) & (holders[None, :] == holders[:, None])
    slot_flat = holders * capacity + jnp.sum(earlier.astype(jnp.int32), axis=1)
    slots = jnp.arange(shards * capacity, dtype=jnp.int32)
    asked = jnp.sum(
        jnp.where(slots[:, None] == slot_flat[None, :], code_flat[None, :], 0), axis=1
    ).reshape(shards, capacity)
    answered = lax.all_to_all(asked, "seq", split_axis=0, concat_axis=0, tiled=True)
    arrived = lax.all_to_all(
        rows_at(table, answered.reshape(shards * capacity)),
        "seq",
        split_axis=0,
        concat_axis=0,
        tiled=True,
    )
    fetched = rows_at(arrived, slot_flat)
    fetched = fetched.reshape(heads_here, blocks_here, RANDOM, BLOCK, 2, DH)
    holder_glob = global_blocks // blocks_here
    place_glob = global_blocks % blocks_here
    mine_glob = holder_glob == my_index
    global_q_local = blocks_at(query_block_tiles, place_glob)
    global_kv_local = blocks_at(own_tiles, place_glob)
    owned_mask = mine_glob.astype(jnp.float32)
    summed_query, summed_pairs = lax.psum(
        (
            global_q_local.astype(jnp.float32) * owned_mask[None, :, None, None],
            global_kv_local.astype(jnp.float32) * owned_mask[None, :, None, None, None],
        ),
        "seq",
    )
    global_query = summed_query.astype(jnp.bfloat16)
    global_pairs = summed_pairs.astype(jnp.bfloat16)
    window = jnp.stack([kv_tiles[:, :-2], kv_tiles[:, 1:-1], kv_tiles[:, 2:]], axis=2)
    spread_global = jnp.broadcast_to(
        global_pairs[:, None], (heads_here, blocks_here, GLOBAL, BLOCK, 2, DH)
    )
    listed = jnp.concatenate([window, fetched, spread_global], axis=2).reshape(
        heads_here, blocks_here, -1, 2, DH
    )
    window_key_rows = listed[:, :, :, 0]
    window_value_rows = listed[:, :, :, 1]
    logit_scores = (
        jnp.einsum(
            "hbqd,hbkd->hbqk",
            query_block_tiles,
            window_key_rows,
            preferred_element_type=jnp.float32,
        )
        * score_multiplier
    )
    column_block = jnp.arange(window_key_rows.shape[2]) // BLOCK
    row_global = my_index * blocks_here + jnp.arange(blocks_here)
    valid_keys = jnp.where(
        column_block[None, :] == 0,
        row_global[:, None] > 0,
        jnp.where(column_block[None, :] == 2, row_global[:, None] < shards * blocks_here - 1, True),
    )
    logit_scores = jnp.where(valid_keys[None, :, None, :], logit_scores, -jnp.inf)
    row_peak = jnp.max(logit_scores, axis=-1, keepdims=True)
    exponent = jnp.exp(logit_scores - row_peak)
    softmax_divisor = jnp.sum(exponent, axis=-1, keepdims=True)
    sparse_result = (
        jnp.einsum(
            "hbqk,hbkd->hbqd",
            exponent.astype(jnp.bfloat16),
            window_value_rows,
            preferred_element_type=jnp.float32,
        )
        / softmax_divisor
    )
    sparse_result = sparse_result.astype(jnp.bfloat16)
    local_keys = own_tiles[:, :, :, 0].reshape(heads_here, tok_rows, DH)
    local_values = own_tiles[:, :, :, 1].reshape(heads_here, tok_rows, DH).astype(jnp.float32)
    global_rows_q = global_query.reshape(heads_here, GLOBAL * BLOCK, DH)
    global_scores = (
        jnp.einsum("hqd,hkd->hqk", global_rows_q, local_keys, preferred_element_type=jnp.float32)
        * score_multiplier
    )
    local_top = jnp.max(global_scores, axis=-1)
    global_exp = jnp.exp(global_scores - local_top[..., None])
    top_all, total_all, out_all = joined(
        (
            local_top,
            jnp.sum(global_exp, axis=-1),
            jnp.einsum("hqk,hkd->hqd", global_exp, local_values, precision=lax.Precision.HIGHEST),
        ),
        "seq",
        combine_parts,
    )
    global_out = (
        (out_all / total_all[..., None]).astype(jnp.bfloat16).reshape(heads_here, GLOBAL, BLOCK, DH)
    )
    block_ids = jnp.arange(blocks_here)
    for glob_index in range(GLOBAL):
        replace_mask = mine_glob[glob_index] & (block_ids == place_glob[glob_index])
        sparse_result = jnp.where(
            replace_mask[None, :, None, None], global_out[:, glob_index][:, None], sparse_result
        )
    attention = sparse_result.transpose(1, 2, 0, 3).reshape(tok_rows, features)
    partial_out = jnp.dot(attention, out_weight, preferred_element_type=jnp.float32)
    return lax.psum_scatter(
        partial_out.astype(jnp.bfloat16), "heads", scatter_dimension=1, tiled=True
    )


MESH = pl.DeviceIdType.MESH
ANY = pl.BlockSpec(memory_space=pl.ANY)
VMEM_BYTES = 56 * 1024 * 1024
SIDE = 2
CORES = 2
TILE = 256


PLAN = ((3, (0,), ()), (4, (1,), ()), (5, (2,), (0,)), (6, (3,), (1,)), (7, (), (2, 3)))


def peers(shards, groups, me, group):
    line = [{"seq": lax.rem(me + k, shards)} for k in range(1, shards)]
    return line + [{"heads": lax.rem(group + k, groups)} for k in range(1, groups)]


def remote(src, dst, send, recv, device):
    return pltpu.make_async_remote_copy(
        src_ref=src,
        dst_ref=dst,
        send_sem=send,
        recv_sem=recv,
        device_id=device,
        device_id_type=MESH,
    )


def crossed(a, b, shards):
    total, bit = 0, 1
    while bit < shards:
        if isinstance(b, int):
            here, there = lax.rem(lax.div(a, bit), 2), (b // bit) % 2
        else:
            here, there = lax.rem(lax.div(a, bit), 2), lax.rem(lax.div(b, bit), 2)
        total = total + bit * (here + there - 2 * here * there)
        bit *= 2
    return total


def layer_kernel(
    shards, heads, groups,
    q_ref, k_ref, v_ref, list_ref, glob_ref, w_ref, out_ref,
    q_here, named, named_near, chosen, glob_all, glob_q, q_all, k_all, v_all, list_all, list_here,
    w_here, glob_here, glob_peak, glob_total, o_here, att, acc,
    send_sem, recv_sem, pass_send, pass_recv, w_send, w_recv, own_sem, glob_send, glob_recv,
    o_send, o_recv, side_send, side_recv, half_send, half_recv,
):
    me = lax.axis_index("seq")
    group = lax.axis_index("heads")
    rows, width = out_ref.shape
    depth = w_ref.shape[0]
    share = CORES
    piece = rows // share
    blocks = rows // BLOCK
    local = blocks // share
    last = shards * blocks - 1
    scale = DH ** (-0.5)
    nt = (((1,), (1,)), ((), ()))
    my_head = lax.div(me, share)
    my_part = lax.rem(me, share)
    partner = my_head * share + (1 - my_part)
    pairs = ((k_ref, k_all), (v_ref, v_all))
    count = len(pairs)

    outer = 1 - lax.rem(my_head + lax.div(my_head, 2), 2)

    def due(t, swapped):
        if isinstance(t, int):
            return t if t < 2 * share else t + swapped * share * (1 - 2 * (t // share % 2))
        far = lax.div(t, 2 * share)
        return t + swapped * far * share * (1 - 2 * lax.rem(lax.div(t, share), 2))

    barrier = pltpu.get_barrier_semaphore()
    known = peers(shards, groups, me, group)
    for device in known:
        pl.semaphore_signal(barrier, inc=1, device_id=device, device_id_type=MESH)

    def window(src, head, part):
        return src.at[
            pl.ds(part * local, local), :, pl.ds(pl.multiple_of(head * DH, DH), DH)
        ]

    def landing(dst, source, part):
        return dst.at[pl.ds(source * blocks + part * local, local)]

    load_q = pltpu.make_async_copy(q_ref, q_here, own_sem.at[0])
    load_q.start()
    own_kv = [
        pltpu.make_async_copy(
            window(src, my_head, my_part), landing(dst, me, my_part), own_sem.at[1 + t]
        )
        for t, (src, dst) in enumerate(pairs)
    ]
    own_q = pltpu.make_async_copy(
        window(q_ref, my_head, my_part), q_all.at[me], own_sem.at[3]
    )
    own_list = pltpu.make_async_copy(list_ref, list_all.at[me], own_sem.at[4])
    own_w = pltpu.make_async_copy(
        w_ref.at[:, pl.ds(pl.multiple_of(group * width, width), width)],
        w_here.at[group],
        own_sem.at[5],
    )
    for copy in (*own_kv, own_q, own_list, own_w):
        copy.start()
    load_q.wait()
    for r in range(GLOBAL):
        picked = q_here[lax.rem(glob_ref[r], blocks)]
        for head in range(heads):
            named[r, head] = picked[:, head * DH : (head + 1) * DH]
    pl.semaphore_wait(barrier, len(known))

    swap = remote(
        named.at[1 - my_part], named_near, glob_send.at[0], glob_recv.at[0], {"seq": partner}
    )
    swap.start()
    sends = {}
    for x in range(1, shards):
        sends[x, count] = remote(
            list_ref,
            list_all.at[me],
            send_sem.at[x, count],
            recv_sem.at[x, count],
            {"seq": crossed(me, x, shards)},
        )
        sends[x, count].start()

    def offer(x):
        to = crossed(me, x, shards)
        head, part = lax.div(to, share), lax.rem(to, share)
        for t, (src, dst) in enumerate(pairs):
            sends[x, t] = remote(
                window(src, head, part),
                landing(dst, me, part),
                send_sem.at[x, t],
                recv_sem.at[x, t],
                {"seq": to},
            )
            sends[x, t].start()

    for x in (2, shards // 2):
        offer(x)
    swap.wait_recv()
    wanted = lax.div(glob_ref[my_part], blocks)
    for head in range(heads):
        apart = jnp.full((BLOCK, DH), wanted, jnp.int32) - jnp.full((BLOCK, DH), partner, jnp.int32)
        chosen[head] = jnp.where(apart == 0, named_near[head], named[my_part, head])
    own_glob = pltpu.make_async_copy(chosen.at[my_head], glob_all.at[my_head], own_sem.at[0])
    own_glob.start()
    globs = {}
    for n in range(1, heads):
        to = crossed(me, n * share, shards)
        globs[n] = remote(
            chosen.at[lax.div(to, share)],
            glob_all.at[my_head],
            glob_send.at[n],
            glob_recv.at[n],
            {"seq": to},
        )
        globs[n].start()
    for x in range(1, shards):
        if x not in (2, shards // 2):
            offer(x)

    def weight_rows(of, part):
        slab = depth // share
        return w_here.at[of, pl.ds(pl.multiple_of(part * slab, slab), slab), :]

    def query(x):
        to = crossed(me, x, shards)
        return remote(
            window(q_ref, lax.div(to, share), lax.rem(to, share)),
            q_all.at[me],
            send_sem.at[x, count + 1],
            recv_sem.at[x, count + 1],
            {"seq": to},
        )

    for x in range(1, share + share):
        query(x).start()

    @pl.when(outer == 0)
    def _():
        for x in range(2 * share, shards - 1):
            query(due(x, outer)).start()

    own_list.wait()
    for x in range(1, shards):
        sends[x, count].wait_recv()
    told = pltpu.make_async_copy(list_all, list_here, own_sem.at[4])
    told.start()
    own_glob.wait()
    for n in range(1, heads):
        globs[n].wait_recv()
    glob_q[my_part] = glob_all[lax.div(wanted, share)]
    glob_pass = remote(
        glob_q.at[my_part], glob_q.at[my_part], glob_send.at[heads], glob_recv.at[heads], {"seq": partner}
    )
    glob_pass.start()
    weights = {}
    for k in range(1, groups):
        to = lax.rem(group + k, groups)
        slab = depth // share
        weights[k] = remote(
            w_ref.at[
                pl.ds(pl.multiple_of(my_part * slab, slab), slab),
                pl.ds(pl.multiple_of(to * width, width), width),
            ],
            weight_rows(group, my_part),
            w_send.at[0, k],
            w_recv.at[0, k],
            {"heads": to},
        )
        weights[k].start()

    told.wait()
    glob_pass.wait_recv()

    def offered(x, t):
        src, dst = pairs[t]
        return remote(
            window(src, 0, 0),
            landing(dst, me, my_part),
            send_sem.at[x, t],
            recv_sem.at[x, t],
            {"seq": crossed(me, x, shards)},
        )

    def handed(x, t):
        region = landing(pairs[t][1], crossed(me, x, shards), my_part)
        return remote(region, region, pass_send.at[x, t], pass_recv.at[x, t], {"seq": partner})

    size = GLOBAL * BLOCK
    glob_peak[...] = jnp.full((size, 1), -jnp.inf, jnp.float32)
    glob_total[...] = jnp.zeros((size, 1), jnp.float32)
    glob_here[...] = jnp.zeros((size, DH), jnp.float32)

    def step(c):
        at = pl.ds(c * blocks, blocks)
        scores = lax.dot_general(
            glob_q[...].reshape(size, DH),
            k_all[at].reshape(rows, DH),
            nt,
            preferred_element_type=jnp.float32,
        ) * scale
        peak = glob_peak[...]
        top = jnp.maximum(peak, jnp.max(scores, axis=-1, keepdims=True))
        fade = jnp.exp(peak - top)
        heavy = jnp.exp(scores - top)
        glob_peak[...] = top
        glob_total[...] = glob_total[...] * fade + jnp.sum(heavy, axis=-1, keepdims=True)
        glob_here[...] = glob_here[...] * fade + jnp.dot(
            heavy.astype(jnp.bfloat16),
            v_all[at].reshape(rows, DH),
            preferred_element_type=jnp.float32,
        )

    @pl.loop(0, heads + 1)
    def _(m):
        @pl.when(m < heads)
        def _():
            for p in range(share):
                x = due(m * share + p, outer)
                for t in range(count):
                    if p == 0:
                        @pl.when(m == 0)
                        def _(t=t):
                            own_kv[t].wait()

                        @pl.when(m > 0)
                        def _(x=x, t=t):
                            offered(x, t).wait_recv()
                    else:
                        offered(x, t).wait_recv()
                    handed(x, t).start()

        @pl.when(m > 0)
        def _():
            for p in range(share):
                for t in range(count):
                    handed(due((m - 1) * share + p, outer), t).wait_recv()
            chip = crossed(my_head, lax.div(due((m - 1) * share, outer), share), heads)
            for p in range(share):
                step(chip * share + p)

    @pl.when(outer == 1)
    def _():
        for x in range(2 * share, shards - 1):
            query(due(x, outer)).start()

    glob_here[...] = glob_here[...] / glob_total[...]
    for k in range(1, groups):
        weights[k].wait_recv()
        of = lax.rem(group + groups - k, groups)
        weights[k, 1] = remote(
            weight_rows(of, my_part),
            weight_rows(of, my_part),
            w_send.at[1, k],
            w_recv.at[1, k],
            {"seq": partner},
        )
        weights[k, 1].start()
    own_q.wait()

    lanes = (3 + RANDOM + GLOBAL) * BLOCK
    column = lax.broadcasted_iota(jnp.int32, (1, lanes), 1) // BLOCK

    def one(i, s, j):
        here = my_part * local + j
        b = s * blocks + here
        listed = [jnp.maximum(b - 1, 0), b, jnp.minimum(b + 1, last)]
        for r in range(RANDOM):
            listed.append(list_here[s, r, my_head, here])
        for r in range(GLOBAL):
            listed.append(glob_ref[r])
        keys = jnp.concatenate([k_all[x] for x in listed], axis=0)
        values = jnp.concatenate([v_all[x] for x in listed], axis=0)
        scores = lax.dot_general(
            q_all[s, j], keys, nt, preferred_element_type=jnp.float32
        ) * scale
        hidden = ((column == 0) & (b == 0)) | ((column == 2) & (b == last))
        scores = jnp.where(hidden, -jnp.inf, scores)
        peak = jnp.max(scores, axis=-1, keepdims=True)
        heavy = jnp.exp(scores - peak)
        total = jnp.sum(heavy, axis=-1, keepdims=True)
        mixed = jnp.dot(heavy.astype(jnp.bfloat16), values, preferred_element_type=jnp.float32)
        result = mixed / total
        for r in range(GLOBAL):
            apart = jnp.full((BLOCK, DH), b, jnp.int32) - jnp.full((BLOCK, DH), glob_ref[r], jnp.int32)
            result = jnp.where(apart == 0, glob_here[r * BLOCK : (r + 1) * BLOCK, :], result)
        o_here[i, j * BLOCK : (j + 1) * BLOCK, :] = result.astype(jnp.bfloat16)

    across = lax.div(group, SIDE)
    along = lax.rem(group, SIDE)
    sides = (across * SIDE + (1 - along), (1 - across) * SIDE + along)
    diagonal = (1 - across) * SIDE + (1 - along)

    def spot(of, source):
        part = lax.rem(source, share)
        return att.at[
            of,
            pl.ds(pl.multiple_of(part * piece, piece), piece),
            pl.ds(pl.multiple_of(lax.div(source, share) * DH, DH), DH),
        ]

    def asked(i):
        return remote(
            window(q_ref, 0, 0),
            q_all.at[me],
            send_sem.at[i, count + 1],
            recv_sem.at[i, count + 1],
            {"seq": crossed(me, i, shards)},
        )

    def kept():
        return pltpu.make_async_copy(o_here.at[0], spot(group, me), own_sem.at[0])

    def back(i):
        return remote(
            o_here.at[i],
            spot(group, me),
            o_send.at[i],
            o_recv.at[i],
            {"seq": crossed(me, i, shards)},
        )

    def sideways(i, n):
        region = spot(group, crossed(me, i, shards))
        return remote(
            region, region, side_send.at[n, i], side_recv.at[n, i], {"heads": sides[n]}
        )

    def corner(i, n):
        half = piece // 2
        region = spot(sides[n], crossed(me, i, shards)).at[n * half : (n + 1) * half, :]
        return remote(
            region, region, half_send.at[n, i], half_recv.at[n, i], {"heads": sides[1 - n]}
        )

    def spread(i):
        if not isinstance(i, int):
            back(i).wait_recv()
        elif i == 0:
            kept().wait()
        else:
            back(i).wait_recv()
        for n in range(SIDE):
            sideways(i, n).start()

    def turn(i):
        for n in range(SIDE):
            sideways(i, n).wait_recv()
            corner(i, n).start()

    def arrive(i):
        for n in range(SIDE):
            corner(i, n).wait_recv()

    @pl.loop(0, shards)
    def _(n):
        i = due(n + share * (1 - 2 * lax.rem(lax.div(n, share), 2)) * (1 - lax.div(n, 2 * share)), outer)
        s = crossed(me, i, shards)

        @pl.when(i > 0)
        def _():
            asked(i).wait_recv()

        for j in range(local):
            one(i, s, j)

        @pl.when(i == 0)
        def _():
            kept().start()

        @pl.when(i > 0)
        def _():
            back(i).start()

        @pl.when(n == 1)
        def _():
            query(due(shards - 1, outer)).start()

        for when, spreads, turns in PLAN:
            @pl.when(n == when)
            def _(spreads=spreads, turns=turns):
                for at in spreads:
                    spread(at)
                for at in turns:
                    turn(at)

    half_depth = depth // 2
    my_side = lax.div(my_head, heads // 2)

    def project(parts, near, slices, first=False, final=False):
        base = (my_side if near else 1 - my_side) * half_depth
        deep = pl.ds(pl.multiple_of(base, half_depth), half_depth)

        for part in slices:
            at = pl.ds(pl.multiple_of(part * piece, piece), piece)

            @pl.loop(0, width // TILE)
            def _(c):
                cols = pl.ds(pl.multiple_of(c * TILE, TILE), TILE)
                term = sum(
                    jnp.dot(
                        att[of, at, deep],
                        w_here[of, deep, cols],
                        preferred_element_type=jnp.float32,
                    )
                    for of in parts
                )
                if not first:
                    term = term + acc[at, cols]
                if final:
                    out_ref[at, cols] = term.astype(out_ref.dtype)
                else:
                    acc[at, cols] = term

    def project_piece(i, parts, final=False):
        source = crossed(me, i, shards)
        at = pl.ds(pl.multiple_of(lax.rem(source, share) * piece, piece), piece)
        deep = pl.ds(pl.multiple_of(lax.div(source, share) * DH, DH), DH)

        @pl.loop(0, width // TILE)
        def _(c):
            cols = pl.ds(pl.multiple_of(c * TILE, TILE), TILE)
            term = acc[at, cols] + jnp.dot(
                jnp.concatenate([att[of, at, deep] for of in parts], axis=1),
                jnp.concatenate([w_here[of, deep, cols] for of in parts], axis=0),
                preferred_element_type=jnp.float32,
            )
            if final:
                out_ref[at, cols] = term.astype(out_ref.dtype)
            else:
                acc[at, cols] = term

    both = (my_part, 1 - my_part)
    ends = (group, diagonal)
    near_end = shards // 2
    own_w.wait()
    for k in range(1, groups):
        weights[k, 1].wait_recv()
    project((group,), True, both, first=True)
    spread(due(near_end, outer))
    for i in range(near_end):
        arrive(i)
    project((*sides, diagonal), True, both)
    for i in range(near_end + 1, shards):
        spread(due(i, outer))
        turn(due(i - 1, outer))
        if i > near_end + 1:
            arrive(due(i - 2, outer))
            project_piece(due(i - 2, outer), sides)
            project_piece(due(i - 2, outer), ends)
    turn(due(shards - 1, outer))
    arrive(due(shards - 2, outer))
    project_piece(due(shards - 2, outer), sides)
    project_piece(due(shards - 2, outer), ends, final=True)
    project_piece(due(shards - 1, outer), sides)
    arrive(due(shards - 1, outer))
    project_piece(due(shards - 1, outer), ends, final=True)

    swap.wait_send()
    glob_pass.wait_send()
    for copy in (*sends.values(), *globs.values(), *weights.values()):
        copy.wait_send()

    @pl.loop(0, shards)
    def _(i):
        for t in range(count):
            handed(i, t).wait_send()

        @pl.when(i > 0)
        def _():
            query(i).wait_send()
            back(i).wait_send()

        for n in range(SIDE):
            sideways(i, n).wait_send()
            corner(i, n).wait_send()


def regrouped(queries, key_vectors, value_vectors, random_blocks, global_blocks, out_weight):
    shards = lax.axis_size("seq")
    groups = lax.axis_size("heads")
    rows, features = queries.shape
    heads = features // DH
    blocks = rows // BLOCK
    piece = rows // CORES
    depth, model = out_weight.shape
    width = model // groups
    lists = random_blocks.transpose(2, 0, 1)
    dma = pltpu.SemaphoreType.DMA
    bf16 = jnp.bfloat16
    whole = pltpu.VMEM((shards * blocks, BLOCK, DH), bf16)
    split = (blocks, BLOCK, features)
    return pl.pallas_call(
        functools.partial(layer_kernel, shards, heads, groups),
        out_shape=pltpu.VMEM((rows, width), bf16),
        in_specs=[ANY] * 4 + [pl.BlockSpec(memory_space=pltpu.SMEM), ANY],
        out_specs=pl.BlockSpec(memory_space=pltpu.VMEM),
        scratch_shapes=[
            pltpu.VMEM(split, bf16),
            pltpu.VMEM((GLOBAL, heads, BLOCK, DH), bf16),
            pltpu.VMEM((heads, BLOCK, DH), bf16),
            pltpu.VMEM((heads, BLOCK, DH), bf16),
            pltpu.VMEM((heads, BLOCK, DH), bf16),
            pltpu.VMEM((GLOBAL, BLOCK, DH), bf16),
            pltpu.VMEM((shards, blocks // CORES, BLOCK, DH), bf16),
            whole,
            whole,
            pltpu.VMEM((shards, *lists.shape), jnp.int32),
            pltpu.SMEM((shards, *lists.shape), jnp.int32),
            pltpu.VMEM((groups, depth, width), bf16),
            pltpu.VMEM((GLOBAL * BLOCK, DH), jnp.float32),
            pltpu.VMEM((GLOBAL * BLOCK, 1), jnp.float32),
            pltpu.VMEM((GLOBAL * BLOCK, 1), jnp.float32),
            pltpu.VMEM((shards, piece, DH), bf16),
            pltpu.VMEM((groups, rows, features), bf16),
            pltpu.VMEM((rows, width), jnp.float32),
            dma((shards, 4)),
            dma((shards, 4)),
            dma((shards, 2)),
            dma((shards, 2)),
            dma((2, groups)),
            dma((2, groups)),
            dma((6,)),
            dma((heads + 1,)),
            dma((heads + 1,)),
            dma((shards,)),
            dma((shards,)),
            dma((SIDE, shards)),
            dma((SIDE, shards)),
            dma((SIDE, shards)),
            dma((SIDE, shards)),
        ],
        compiler_params=pltpu.CompilerParams(
            collective_id=0, has_side_effects=True, vmem_limit_bytes=VMEM_BYTES
        ),
        name="layer",
    )(
        queries.reshape(split),
        key_vectors.reshape(split),
        value_vectors.reshape(split),
        lists,
        global_blocks,
        out_weight,
    )


def on_device(queries, key_vectors, value_vectors, random_blocks, global_blocks, out_weight):
    shards = lax.axis_size("seq")
    groups = lax.axis_size("heads")
    rows, features = queries.shape
    heads = features // DH
    fits = shards == heads * CORES and heads == 4 and groups == SIDE * SIDE and GLOBAL == CORES
    body = regrouped if fits and (rows // BLOCK) % CORES == 0 else requested
    return body(queries, key_vectors, value_vectors, random_blocks, global_blocks, out_weight)


def solution(mesh):
    placed = (
        P("seq", "heads"),
        P("seq", "heads"),
        P("seq", "heads"),
        P("heads", "seq", None),
        P(),
        P("heads", None),
    )
    return jax.shard_map(
        on_device, mesh=mesh, in_specs=placed, out_specs=P("seq", "heads"), check_vma=False
    )
```

```python
import functools

import jax
import jax.numpy as jnp
from jax import lax
from jax.experimental import pallas as pl
from jax.experimental.pallas import tpu as pltpu
from jax.sharding import PartitionSpec as P

DH = 128
BLOCK = 64
RANDOM = 3
GLOBAL = 2


def extended(shard, sides, width):
    for axis, dim in sides:
        peers, length = (lax.axis_size(axis), shard.shape[dim])
        up = [(i, (i + 1) % peers) for i in range(peers - 1)]
        down = [(j, i) for i, j in up]
        last = lax.slice_in_dim(shard, length - width, length, axis=dim)
        leading = lax.slice_in_dim(shard, 0, width, axis=dim)
        before = lax.ppermute(last, axis, up)
        after = lax.ppermute(leading, axis, down)
        shard = jnp.concatenate([before, shard, after], axis=dim)
    return shard


def joined(shard, axis, combine):
    everything = jax.tree.map(
        lambda part, kind: lax.all_gather(part.astype(kind), axis),
        shard,
        (jnp.bfloat16, jnp.bfloat16, jnp.bfloat16),
    )

    def take(k):
        return jax.tree.map(lambda part, own: part[k].astype(own.dtype), everything, shard)

    return lax.fori_loop(
        1, lax.axis_size(axis), lambda k, so_far: combine(so_far, take(k)), take(0)
    )


def combine_parts(first, second):
    top_first, total_first, out_first = first
    top_second, total_second, out_second = second
    highest = jnp.maximum(top_first, top_second)
    scale_first = jnp.exp(top_first - highest)
    scale_second = jnp.exp(top_second - highest)
    return (
        highest,
        total_first * scale_first + total_second * scale_second,
        out_first * scale_first[..., None] + out_second * scale_second[..., None],
    )


def rows_at(table, index):
    chosen = (index[:, None] == jnp.arange(table.shape[0], dtype=jnp.int32)[None, :]).astype(table.dtype)
    return jnp.dot(chosen, table, preferred_element_type=jnp.float32).astype(table.dtype)


def blocks_at(tiles, index):
    return jnp.stack([lax.dynamic_index_in_dim(tiles, index[r], 1, False) for r in range(GLOBAL)], axis=1)


def requested(queries, key_vectors, value_vectors, random_blocks, global_blocks, out_weight):
    shards = lax.axis_size("seq")
    my_index = lax.axis_index("seq")
    tok_rows, features = queries.shape
    heads_here = features // DH
    blocks_here = tok_rows // BLOCK
    requests = heads_here * blocks_here * RANDOM
    capacity = max(2, 3 * requests // (2 * shards) + 1)
    score_multiplier = DH ** (-0.5)
    query_block_tiles = queries.reshape(blocks_here, BLOCK, heads_here, DH).transpose(2, 0, 1, 3)
    stacked = jnp.concatenate([key_vectors, value_vectors], axis=1)
    padded = extended(stacked, (("seq", 0),), BLOCK)
    kv_tiles = padded.reshape(blocks_here + 2, BLOCK, 2, heads_here, DH).transpose(3, 0, 1, 2, 4)
    own_tiles = kv_tiles[:, 1:-1]
    table = own_tiles.reshape(heads_here * blocks_here, BLOCK * 2 * DH)
    flat_lists = random_blocks.reshape(requests)
    head_of = jnp.arange(requests, dtype=jnp.int32) // (blocks_here * RANDOM)
    code_flat = head_of * blocks_here + flat_lists % blocks_here
    holders = flat_lists // blocks_here
    order = jnp.arange(requests, dtype=jnp.int32)
    earlier = (order[None, :] < order[:, None]) & (holders[None, :] == holders[:, None])
    slot_flat = holders * capacity + jnp.sum(earlier.astype(jnp.int32), axis=1)
    slots = jnp.arange(shards * capacity, dtype=jnp.int32)
    asked = jnp.sum(
        jnp.where(slots[:, None] == slot_flat[None, :], code_flat[None, :], 0), axis=1
    ).reshape(shards, capacity)
    answered = lax.all_to_all(asked, "seq", split_axis=0, concat_axis=0, tiled=True)
    arrived = lax.all_to_all(
        rows_at(table, answered.reshape(shards * capacity)),
        "seq",
        split_axis=0,
        concat_axis=0,
        tiled=True,
    )
    fetched = rows_at(arrived, slot_flat)
    fetched = fetched.reshape(heads_here, blocks_here, RANDOM, BLOCK, 2, DH)
    holder_glob = global_blocks // blocks_here
    place_glob = global_blocks % blocks_here
    mine_glob = holder_glob == my_index
    global_q_local = blocks_at(query_block_tiles, place_glob)
    global_kv_local = blocks_at(own_tiles, place_glob)
    owned_mask = mine_glob.astype(jnp.float32)
    summed_query, summed_pairs = lax.psum(
        (
            global_q_local.astype(jnp.float32) * owned_mask[None, :, None, None],
            global_kv_local.astype(jnp.float32) * owned_mask[None, :, None, None, None],
        ),
        "seq",
    )
    global_query = summed_query.astype(jnp.bfloat16)
    global_pairs = summed_pairs.astype(jnp.bfloat16)
    window = jnp.stack([kv_tiles[:, :-2], kv_tiles[:, 1:-1], kv_tiles[:, 2:]], axis=2)
    spread_global = jnp.broadcast_to(
        global_pairs[:, None], (heads_here, blocks_here, GLOBAL, BLOCK, 2, DH)
    )
    listed = jnp.concatenate([window, fetched, spread_global], axis=2).reshape(
        heads_here, blocks_here, -1, 2, DH
    )
    window_key_rows = listed[:, :, :, 0]
    window_value_rows = listed[:, :, :, 1]
    logit_scores = (
        jnp.einsum(
            "hbqd,hbkd->hbqk",
            query_block_tiles,
            window_key_rows,
            preferred_element_type=jnp.float32,
        )
        * score_multiplier
    )
    column_block = jnp.arange(window_key_rows.shape[2]) // BLOCK
    row_global = my_index * blocks_here + jnp.arange(blocks_here)
    valid_keys = jnp.where(
        column_block[None, :] == 0,
        row_global[:, None] > 0,
        jnp.where(column_block[None, :] == 2, row_global[:, None] < shards * blocks_here - 1, True),
    )
    logit_scores = jnp.where(valid_keys[None, :, None, :], logit_scores, -jnp.inf)
    row_peak = jnp.max(logit_scores, axis=-1, keepdims=True)
    exponent = jnp.exp(logit_scores - row_peak)
    softmax_divisor = jnp.sum(exponent, axis=-1, keepdims=True)
    sparse_result = (
        jnp.einsum(
            "hbqk,hbkd->hbqd",
            exponent.astype(jnp.bfloat16),
            window_value_rows,
            preferred_element_type=jnp.float32,
        )
        / softmax_divisor
    )
    sparse_result = sparse_result.astype(jnp.bfloat16)
    local_keys = own_tiles[:, :, :, 0].reshape(heads_here, tok_rows, DH)
    local_values = own_tiles[:, :, :, 1].reshape(heads_here, tok_rows, DH).astype(jnp.float32)
    global_rows_q = global_query.reshape(heads_here, GLOBAL * BLOCK, DH)
    global_scores = (
        jnp.einsum("hqd,hkd->hqk", global_rows_q, local_keys, preferred_element_type=jnp.float32)
        * score_multiplier
    )
    local_top = jnp.max(global_scores, axis=-1)
    global_exp = jnp.exp(global_scores - local_top[..., None])
    top_all, total_all, out_all = joined(
        (
            local_top,
            jnp.sum(global_exp, axis=-1),
            jnp.einsum("hqk,hkd->hqd", global_exp, local_values, precision=lax.Precision.HIGHEST),
        ),
        "seq",
        combine_parts,
    )
    global_out = (
        (out_all / total_all[..., None]).astype(jnp.bfloat16).reshape(heads_here, GLOBAL, BLOCK, DH)
    )
    block_ids = jnp.arange(blocks_here)
    for glob_index in range(GLOBAL):
        replace_mask = mine_glob[glob_index] & (block_ids == place_glob[glob_index])
        sparse_result = jnp.where(
            replace_mask[None, :, None, None], global_out[:, glob_index][:, None], sparse_result
        )
    attention = sparse_result.transpose(1, 2, 0, 3).reshape(tok_rows, features)
    partial_out = jnp.dot(attention, out_weight, preferred_element_type=jnp.float32)
    return lax.psum_scatter(
        partial_out.astype(jnp.bfloat16), "heads", scatter_dimension=1, tiled=True
    )


MESH = pl.DeviceIdType.MESH
ANY = pl.BlockSpec(memory_space=pl.ANY)
VMEM_BYTES = 56 * 1024 * 1024
SIDE = 2
CORES = 2
TILE = 1024


PLAN = ((3, (0,), ()), (4, (1,), ()), (5, (2,), (0,)), (6, (3,), (1,)), (7, (), (2, 3)))


def peers(shards, groups, me, group):
    line = [{"seq": lax.rem(me + k, shards)} for k in range(1, shards)]
    return line + [{"heads": lax.rem(group + k, groups)} for k in range(1, groups)]


def remote(src, dst, send, recv, device):
    return pltpu.make_async_remote_copy(
        src_ref=src,
        dst_ref=dst,
        send_sem=send,
        recv_sem=recv,
        device_id=device,
        device_id_type=MESH,
    )


def crossed(a, b, shards):
    total, bit = 0, 1
    while bit < shards:
        if isinstance(b, int):
            here, there = lax.rem(lax.div(a, bit), 2), (b // bit) % 2
        else:
            here, there = lax.rem(lax.div(a, bit), 2), lax.rem(lax.div(b, bit), 2)
        total = total + bit * (here + there - 2 * here * there)
        bit *= 2
    return total


def layer_kernel(
    shards, heads, groups,
    q_ref, k_ref, v_ref, list_ref, glob_ref, w_ref, out_ref,
    q_here, named, named_near, chosen, glob_all, glob_q, q_all, k_all, v_all, list_all, list_here,
    w_here, glob_here, glob_peak, glob_total, o_here, att, acc,
    send_sem, recv_sem, pass_send, pass_recv, w_send, w_recv, own_sem, glob_send, glob_recv,
    o_send, o_recv, side_send, side_recv, half_send, half_recv,
):
    me = lax.axis_index("seq")
    group = lax.axis_index("heads")
    rows, width = out_ref.shape
    depth = w_ref.shape[0]
    share = CORES
    piece = rows // share
    blocks = rows // BLOCK
    local = blocks // share
    last = shards * blocks - 1
    scale = DH ** (-0.5)
    nt = (((1,), (1,)), ((), ()))
    my_head = lax.div(me, share)
    my_part = lax.rem(me, share)
    partner = my_head * share + (1 - my_part)
    pairs = ((k_ref, k_all), (v_ref, v_all))
    count = len(pairs)

    outer = 1 - lax.rem(my_head + lax.div(my_head, 2), 2)

    def due(t, swapped):
        if isinstance(t, int):
            return t if t < 2 * share else t + swapped * share * (1 - 2 * (t // share % 2))
        far = lax.div(t, 2 * share)
        return t + swapped * far * share * (1 - 2 * lax.rem(lax.div(t, share), 2))

    barrier = pltpu.get_barrier_semaphore()
    known = peers(shards, groups, me, group)
    for device in known:
        pl.semaphore_signal(barrier, inc=1, device_id=device, device_id_type=MESH)

    def window(src, head, part):
        return src.at[
            pl.ds(part * local, local), :, pl.ds(pl.multiple_of(head * DH, DH), DH)
        ]

    def landing(dst, source, part):
        return dst.at[pl.ds(source * blocks + part * local, local)]

    load_q = pltpu.make_async_copy(q_ref, q_here, own_sem.at[0])
    load_q.start()
    own_kv = [
        pltpu.make_async_copy(
            window(src, my_head, my_part), landing(dst, me, my_part), own_sem.at[1 + t]
        )
        for t, (src, dst) in enumerate(pairs)
    ]
    own_q = pltpu.make_async_copy(
        window(q_ref, my_head, my_part), q_all.at[me], own_sem.at[3]
    )
    own_list = pltpu.make_async_copy(list_ref, list_all.at[me], own_sem.at[4])
    own_w = pltpu.make_async_copy(
        w_ref.at[:, pl.ds(pl.multiple_of(group * width, width), width)],
        w_here.at[group],
        own_sem.at[5],
    )
    for copy in (*own_kv, own_q, own_list, own_w):
        copy.start()
    load_q.wait()
    for r in range(GLOBAL):
        picked = q_here[lax.rem(glob_ref[r], blocks)]
        for head in range(heads):
            named[r, head] = picked[:, head * DH : (head + 1) * DH]
    pl.semaphore_wait(barrier, len(known))

    swap = remote(
        named.at[1 - my_part], named_near, glob_send.at[0], glob_recv.at[0], {"seq": partner}
    )
    swap.start()
    sends = {}
    for x in range(1, shards):
        sends[x, count] = remote(
            list_ref,
            list_all.at[me],
            send_sem.at[x, count],
            recv_sem.at[x, count],
            {"seq": crossed(me, x, shards)},
        )
        sends[x, count].start()

    def offer(x):
        to = crossed(me, x, shards)
        head, part = lax.div(to, share), lax.rem(to, share)
        for t, (src, dst) in enumerate(pairs):
            sends[x, t] = remote(
                window(src, head, part),
                landing(dst, me, part),
                send_sem.at[x, t],
                recv_sem.at[x, t],
                {"seq": to},
            )
            sends[x, t].start()

    for x in (2, shards // 2):
        offer(x)
    swap.wait_recv()
    wanted = lax.div(glob_ref[my_part], blocks)
    for head in range(heads):
        apart = jnp.full((BLOCK, DH), wanted, jnp.int32) - jnp.full((BLOCK, DH), partner, jnp.int32)
        chosen[head] = jnp.where(apart == 0, named_near[head], named[my_part, head])
    own_glob = pltpu.make_async_copy(chosen.at[my_head], glob_all.at[my_head], own_sem.at[0])
    own_glob.start()
    globs = {}
    for n in range(1, heads):
        to = crossed(me, n * share, shards)
        globs[n] = remote(
            chosen.at[lax.div(to, share)],
            glob_all.at[my_head],
            glob_send.at[n],
            glob_recv.at[n],
            {"seq": to},
        )
        globs[n].start()
    for x in range(1, shards):
        if x not in (2, shards // 2):
            offer(x)

    def weight_rows(of, part):
        slab = depth // share
        return w_here.at[of, pl.ds(pl.multiple_of(part * slab, slab), slab), :]

    def query(x):
        to = crossed(me, x, shards)
        return remote(
            window(q_ref, lax.div(to, share), lax.rem(to, share)),
            q_all.at[me],
            send_sem.at[x, count + 1],
            recv_sem.at[x, count + 1],
            {"seq": to},
        )

    for x in range(1, share + share):
        query(x).start()

    @pl.when(outer == 0)
    def _():
        for x in range(2 * share, shards - 2):
            query(due(x, outer)).start()

    own_list.wait()
    for x in range(1, shards):
        sends[x, count].wait_recv()
    told = pltpu.make_async_copy(list_all, list_here, own_sem.at[4])
    told.start()
    own_glob.wait()
    for n in range(1, heads):
        globs[n].wait_recv()
    glob_q[my_part] = glob_all[lax.div(wanted, share)]
    glob_pass = remote(
        glob_q.at[my_part], glob_q.at[my_part], glob_send.at[heads], glob_recv.at[heads], {"seq": partner}
    )
    glob_pass.start()
    weights = {}
    for k in range(1, groups):
        to = lax.rem(group + k, groups)
        slab = depth // share
        weights[k] = remote(
            w_ref.at[
                pl.ds(pl.multiple_of(my_part * slab, slab), slab),
                pl.ds(pl.multiple_of(to * width, width), width),
            ],
            weight_rows(group, my_part),
            w_send.at[0, k],
            w_recv.at[0, k],
            {"heads": to},
        )
        weights[k].start()

    told.wait()
    glob_pass.wait_recv()

    def offered(x, t):
        src, dst = pairs[t]
        return remote(
            window(src, 0, 0),
            landing(dst, me, my_part),
            send_sem.at[x, t],
            recv_sem.at[x, t],
            {"seq": crossed(me, x, shards)},
        )

    def handed(x, t):
        region = landing(pairs[t][1], crossed(me, x, shards), my_part)
        return remote(region, region, pass_send.at[x, t], pass_recv.at[x, t], {"seq": partner})

    size = GLOBAL * BLOCK
    glob_peak[...] = jnp.full((size, 1), -jnp.inf, jnp.float32)
    glob_total[...] = jnp.zeros((size, 1), jnp.float32)
    glob_here[...] = jnp.zeros((size, DH), jnp.float32)

    def step(c):
        at = pl.ds(c * blocks, blocks)
        scores = lax.dot_general(
            glob_q[...].reshape(size, DH),
            k_all[at].reshape(rows, DH),
            nt,
            preferred_element_type=jnp.float32,
        ) * scale
        peak = glob_peak[...]
        top = jnp.maximum(peak, jnp.max(scores, axis=-1, keepdims=True))
        fade = jnp.exp(peak - top)
        heavy = jnp.exp(scores - top)
        glob_peak[...] = top
        glob_total[...] = glob_total[...] * fade + jnp.sum(heavy, axis=-1, keepdims=True)
        glob_here[...] = glob_here[...] * fade + jnp.dot(
            heavy.astype(jnp.bfloat16),
            v_all[at].reshape(rows, DH),
            preferred_element_type=jnp.float32,
        )

    @pl.loop(0, heads + 1)
    def _(m):
        @pl.when(m < heads)
        def _():
            for p in range(share):
                x = due(m * share + p, outer)
                for t in range(count):
                    if p == 0:
                        @pl.when(m == 0)
                        def _(t=t):
                            own_kv[t].wait()

                        @pl.when(m > 0)
                        def _(x=x, t=t):
                            offered(x, t).wait_recv()
                    else:
                        offered(x, t).wait_recv()
                    handed(x, t).start()

        @pl.when(m > 0)
        def _():
            for p in range(share):
                for t in range(count):
                    handed(due((m - 1) * share + p, outer), t).wait_recv()
            chip = crossed(my_head, lax.div(due((m - 1) * share, outer), share), heads)
            for p in range(share):
                step(chip * share + p)

    @pl.when(outer == 1)
    def _():
        for x in range(2 * share, shards - 2):
            query(due(x, outer)).start()

    glob_here[...] = glob_here[...] / glob_total[...]
    for k in range(1, groups):
        weights[k].wait_recv()
        of = lax.rem(group + groups - k, groups)
        weights[k, 1] = remote(
            weight_rows(of, my_part),
            weight_rows(of, my_part),
            w_send.at[1, k],
            w_recv.at[1, k],
            {"seq": partner},
        )
        weights[k, 1].start()
    own_q.wait()

    lanes = (3 + RANDOM + GLOBAL) * BLOCK
    column = lax.broadcasted_iota(jnp.int32, (1, lanes), 1) // BLOCK

    def one(i, s, j):
        here = my_part * local + j
        b = s * blocks + here
        listed = [jnp.maximum(b - 1, 0), b, jnp.minimum(b + 1, last)]
        for r in range(RANDOM):
            listed.append(list_here[s, r, my_head, here])
        for r in range(GLOBAL):
            listed.append(glob_ref[r])
        keys = jnp.concatenate([k_all[x] for x in listed], axis=0)
        values = jnp.concatenate([v_all[x] for x in listed], axis=0)
        scores = lax.dot_general(
            q_all[s, j], keys, nt, preferred_element_type=jnp.float32
        ) * scale
        hidden = ((column == 0) & (b == 0)) | ((column == 2) & (b == last))
        scores = jnp.where(hidden, -jnp.inf, scores)
        peak = jnp.max(scores, axis=-1, keepdims=True)
        heavy = jnp.exp(scores - peak)
        total = jnp.sum(heavy, axis=-1, keepdims=True)
        mixed = jnp.dot(heavy.astype(jnp.bfloat16), values, preferred_element_type=jnp.float32)
        result = mixed / total
        for r in range(GLOBAL):
            apart = jnp.full((BLOCK, DH), b, jnp.int32) - jnp.full((BLOCK, DH), glob_ref[r], jnp.int32)
            result = jnp.where(apart == 0, glob_here[r * BLOCK : (r + 1) * BLOCK, :], result)
        o_here[i, j * BLOCK : (j + 1) * BLOCK, :] = result.astype(jnp.bfloat16)

    across = lax.div(group, SIDE)
    along = lax.rem(group, SIDE)
    sides = (across * SIDE + (1 - along), (1 - across) * SIDE + along)
    diagonal = (1 - across) * SIDE + (1 - along)

    def spot(of, source):
        part = lax.rem(source, share)
        return att.at[
            of,
            pl.ds(pl.multiple_of(part * piece, piece), piece),
            pl.ds(pl.multiple_of(lax.div(source, share) * DH, DH), DH),
        ]

    def asked(i):
        return remote(
            window(q_ref, 0, 0),
            q_all.at[me],
            send_sem.at[i, count + 1],
            recv_sem.at[i, count + 1],
            {"seq": crossed(me, i, shards)},
        )

    def kept():
        return pltpu.make_async_copy(o_here.at[0], spot(group, me), own_sem.at[0])

    def back(i):
        return remote(
            o_here.at[i],
            spot(group, me),
            o_send.at[i],
            o_recv.at[i],
            {"seq": crossed(me, i, shards)},
        )

    def sideways(i, n):
        region = spot(group, crossed(me, i, shards))
        return remote(
            region, region, side_send.at[n, i], side_recv.at[n, i], {"heads": sides[n]}
        )

    def corner(i, n):
        half = piece // 2
        region = spot(sides[n], crossed(me, i, shards)).at[n * half : (n + 1) * half, :]
        return remote(
            region, region, half_send.at[n, i], half_recv.at[n, i], {"heads": sides[1 - n]}
        )

    def spread(i):
        if not isinstance(i, int):
            back(i).wait_recv()
        elif i == 0:
            kept().wait()
        else:
            back(i).wait_recv()
        for n in range(SIDE):
            sideways(i, n).start()

    def turn(i):
        for n in range(SIDE):
            sideways(i, n).wait_recv()
            corner(i, n).start()

    def arrive(i):
        for n in range(SIDE):
            corner(i, n).wait_recv()

    @pl.loop(0, shards)
    def _(n):
        i = due(n + share * (1 - 2 * lax.rem(lax.div(n, share), 2)) * (1 - lax.div(n, 2 * share)), outer)
        s = crossed(me, i, shards)

        @pl.when(i > 0)
        def _():
            asked(i).wait_recv()

        for j in range(local):
            one(i, s, j)

        @pl.when(i == 0)
        def _():
            kept().start()

        @pl.when(i > 0)
        def _():
            back(i).start()

        @pl.when(n == 1)
        def _():
            query(due(shards - 2, outer)).start()

        @pl.when(n == 3)
        def _():
            query(due(shards - 1, outer)).start()

        for when, spreads, turns in PLAN:
            @pl.when(n == when)
            def _(spreads=spreads, turns=turns):
                for at in spreads:
                    spread(at)
                for at in turns:
                    turn(at)

    half_depth = depth // 2
    my_side = lax.div(my_head, heads // 2)

    def project(parts, near, slices, first=False, final=False):
        base = (my_side if near else 1 - my_side) * half_depth
        deep = pl.ds(pl.multiple_of(base, half_depth), half_depth)

        for part in slices:
            at = pl.ds(pl.multiple_of(part * piece, piece), piece)

            @pl.loop(0, width // TILE)
            def _(c):
                cols = pl.ds(pl.multiple_of(c * TILE, TILE), TILE)
                term = sum(
                    jnp.dot(
                        att[of, at, deep],
                        w_here[of, deep, cols],
                        preferred_element_type=jnp.float32,
                    )
                    for of in parts
                )
                if not first:
                    term = term + acc[at, cols]
                if final:
                    out_ref[at, cols] = term.astype(out_ref.dtype)
                else:
                    acc[at, cols] = term

    def project_piece(i, parts, final=False):
        source = crossed(me, i, shards)
        at = pl.ds(pl.multiple_of(lax.rem(source, share) * piece, piece), piece)
        deep = pl.ds(pl.multiple_of(lax.div(source, share) * DH, DH), DH)

        @pl.loop(0, width // TILE)
        def _(c):
            cols = pl.ds(pl.multiple_of(c * TILE, TILE), TILE)
            term = acc[at, cols] + jnp.dot(
                jnp.concatenate([att[of, at, deep] for of in parts], axis=1),
                jnp.concatenate([w_here[of, deep, cols] for of in parts], axis=0),
                preferred_element_type=jnp.float32,
            )
            if final:
                out_ref[at, cols] = term.astype(out_ref.dtype)
            else:
                acc[at, cols] = term

    both = (my_part, 1 - my_part)
    ends = (group, diagonal)
    near_end = shards // 2
    own_w.wait()
    for k in range(1, groups):
        weights[k, 1].wait_recv()
    project((group,), True, both, first=True)
    spread(due(near_end, outer))

    @pl.when(outer == 1)
    def _():
        spread(due(near_end + 1, outer))
        turn(due(near_end, outer))

    for i in range(near_end):
        arrive(i)
    project((*sides, diagonal), True, both)

    @pl.when(outer == 0)
    def _():
        spread(due(near_end + 1, outer))
        turn(due(near_end, outer))

    for i in range(near_end + 2, shards):
        spread(due(i, outer))
        turn(due(i - 1, outer))
        arrive(due(i - 2, outer))
        project_piece(due(i - 2, outer), sides)
        project_piece(due(i - 2, outer), ends)
    turn(due(shards - 1, outer))
    arrive(due(shards - 2, outer))
    project_piece(due(shards - 2, outer), sides)
    project_piece(due(shards - 2, outer), ends, final=True)
    project_piece(due(shards - 1, outer), sides)
    arrive(due(shards - 1, outer))
    project_piece(due(shards - 1, outer), ends, final=True)

    swap.wait_send()
    glob_pass.wait_send()
    for copy in (*sends.values(), *globs.values(), *weights.values()):
        copy.wait_send()

    @pl.loop(0, shards)
    def _(i):
        for t in range(count):
            handed(i, t).wait_send()

        @pl.when(i > 0)
        def _():
            query(i).wait_send()
            back(i).wait_send()

        for n in range(SIDE):
            sideways(i, n).wait_send()
            corner(i, n).wait_send()


def regrouped(queries, key_vectors, value_vectors, random_blocks, global_blocks, out_weight):
    shards = lax.axis_size("seq")
    groups = lax.axis_size("heads")
    rows, features = queries.shape
    heads = features // DH
    blocks = rows // BLOCK
    piece = rows // CORES
    depth, model = out_weight.shape
    width = model // groups
    lists = random_blocks.transpose(2, 0, 1)
    dma = pltpu.SemaphoreType.DMA
    bf16 = jnp.bfloat16
    whole = pltpu.VMEM((shards * blocks, BLOCK, DH), bf16)
    split = (blocks, BLOCK, features)
    return pl.pallas_call(
        functools.partial(layer_kernel, shards, heads, groups),
        out_shape=pltpu.VMEM((rows, width), bf16),
        in_specs=[ANY] * 4 + [pl.BlockSpec(memory_space=pltpu.SMEM), ANY],
        out_specs=pl.BlockSpec(memory_space=pltpu.VMEM),
        scratch_shapes=[
            pltpu.VMEM(split, bf16),
            pltpu.VMEM((GLOBAL, heads, BLOCK, DH), bf16),
            pltpu.VMEM((heads, BLOCK, DH), bf16),
            pltpu.VMEM((heads, BLOCK, DH), bf16),
            pltpu.VMEM((heads, BLOCK, DH), bf16),
            pltpu.VMEM((GLOBAL, BLOCK, DH), bf16),
            pltpu.VMEM((shards, blocks // CORES, BLOCK, DH), bf16),
            whole,
            whole,
            pltpu.VMEM((shards, *lists.shape), jnp.int32),
            pltpu.SMEM((shards, *lists.shape), jnp.int32),
            pltpu.VMEM((groups, depth, width), bf16),
            pltpu.VMEM((GLOBAL * BLOCK, DH), jnp.float32),
            pltpu.VMEM((GLOBAL * BLOCK, 1), jnp.float32),
            pltpu.VMEM((GLOBAL * BLOCK, 1), jnp.float32),
            pltpu.VMEM((shards, piece, DH), bf16),
            pltpu.VMEM((groups, rows, features), bf16),
            pltpu.VMEM((rows, width), jnp.float32),
            dma((shards, 4)),
            dma((shards, 4)),
            dma((shards, 2)),
            dma((shards, 2)),
            dma((2, groups)),
            dma((2, groups)),
            dma((6,)),
            dma((heads + 1,)),
            dma((heads + 1,)),
            dma((shards,)),
            dma((shards,)),
            dma((SIDE, shards)),
            dma((SIDE, shards)),
            dma((SIDE, shards)),
            dma((SIDE, shards)),
        ],
        compiler_params=pltpu.CompilerParams(
            collective_id=0, has_side_effects=True, vmem_limit_bytes=VMEM_BYTES
        ),
        name="layer",
    )(
        queries.reshape(split),
        key_vectors.reshape(split),
        value_vectors.reshape(split),
        lists,
        global_blocks,
        out_weight,
    )


def on_device(queries, key_vectors, value_vectors, random_blocks, global_blocks, out_weight):
    shards = lax.axis_size("seq")
    groups = lax.axis_size("heads")
    rows, features = queries.shape
    heads = features // DH
    fits = shards == heads * CORES and heads == 4 and groups == SIDE * SIDE and GLOBAL == CORES
    fits = fits and (out_weight.shape[1] // groups) % TILE == 0
    body = regrouped if fits and (rows // BLOCK) % CORES == 0 else requested
    return body(queries, key_vectors, value_vectors, random_blocks, global_blocks, out_weight)


def solution(mesh):
    placed = (
        P("seq", "heads"),
        P("seq", "heads"),
        P("seq", "heads"),
        P("heads", "seq", None),
        P(),
        P("heads", None),
    )
    return jax.shard_map(
        on_device, mesh=mesh, in_specs=placed, out_specs=P("seq", "heads"), check_vma=False
    )
```

```python
import functools

import jax
import jax.numpy as jnp
from jax import lax
from jax.experimental import pallas as pl
from jax.experimental.pallas import tpu as pltpu
from jax.sharding import PartitionSpec as P

DH = 128
BLOCK = 64
RANDOM = 3
GLOBAL = 2


def extended(shard, sides, width):
    for axis, dim in sides:
        peers, length = (lax.axis_size(axis), shard.shape[dim])
        up = [(i, (i + 1) % peers) for i in range(peers - 1)]
        down = [(j, i) for i, j in up]
        last = lax.slice_in_dim(shard, length - width, length, axis=dim)
        leading = lax.slice_in_dim(shard, 0, width, axis=dim)
        before = lax.ppermute(last, axis, up)
        after = lax.ppermute(leading, axis, down)
        shard = jnp.concatenate([before, shard, after], axis=dim)
    return shard


def joined(shard, axis, combine):
    everything = jax.tree.map(
        lambda part, kind: lax.all_gather(part.astype(kind), axis),
        shard,
        (jnp.bfloat16, jnp.bfloat16, jnp.bfloat16),
    )

    def take(k):
        return jax.tree.map(lambda part, own: part[k].astype(own.dtype), everything, shard)

    return lax.fori_loop(
        1, lax.axis_size(axis), lambda k, so_far: combine(so_far, take(k)), take(0)
    )


def combine_parts(first, second):
    top_first, total_first, out_first = first
    top_second, total_second, out_second = second
    highest = jnp.maximum(top_first, top_second)
    scale_first = jnp.exp(top_first - highest)
    scale_second = jnp.exp(top_second - highest)
    return (
        highest,
        total_first * scale_first + total_second * scale_second,
        out_first * scale_first[..., None] + out_second * scale_second[..., None],
    )


def rows_at(table, index):
    chosen = (index[:, None] == jnp.arange(table.shape[0], dtype=jnp.int32)[None, :]).astype(table.dtype)
    return jnp.dot(chosen, table, preferred_element_type=jnp.float32).astype(table.dtype)


def blocks_at(tiles, index):
    return jnp.stack([lax.dynamic_index_in_dim(tiles, index[r], 1, False) for r in range(GLOBAL)], axis=1)


def requested(queries, key_vectors, value_vectors, random_blocks, global_blocks, out_weight):
    shards = lax.axis_size("seq")
    my_index = lax.axis_index("seq")
    tok_rows, features = queries.shape
    heads_here = features // DH
    blocks_here = tok_rows // BLOCK
    requests = heads_here * blocks_here * RANDOM
    capacity = max(2, 3 * requests // (2 * shards) + 1)
    score_multiplier = DH ** (-0.5)
    query_block_tiles = queries.reshape(blocks_here, BLOCK, heads_here, DH).transpose(2, 0, 1, 3)
    stacked = jnp.concatenate([key_vectors, value_vectors], axis=1)
    padded = extended(stacked, (("seq", 0),), BLOCK)
    kv_tiles = padded.reshape(blocks_here + 2, BLOCK, 2, heads_here, DH).transpose(3, 0, 1, 2, 4)
    own_tiles = kv_tiles[:, 1:-1]
    table = own_tiles.reshape(heads_here * blocks_here, BLOCK * 2 * DH)
    flat_lists = random_blocks.reshape(requests)
    head_of = jnp.arange(requests, dtype=jnp.int32) // (blocks_here * RANDOM)
    code_flat = head_of * blocks_here + flat_lists % blocks_here
    holders = flat_lists // blocks_here
    order = jnp.arange(requests, dtype=jnp.int32)
    earlier = (order[None, :] < order[:, None]) & (holders[None, :] == holders[:, None])
    slot_flat = holders * capacity + jnp.sum(earlier.astype(jnp.int32), axis=1)
    slots = jnp.arange(shards * capacity, dtype=jnp.int32)
    asked = jnp.sum(
        jnp.where(slots[:, None] == slot_flat[None, :], code_flat[None, :], 0), axis=1
    ).reshape(shards, capacity)
    answered = lax.all_to_all(asked, "seq", split_axis=0, concat_axis=0, tiled=True)
    arrived = lax.all_to_all(
        rows_at(table, answered.reshape(shards * capacity)),
        "seq",
        split_axis=0,
        concat_axis=0,
        tiled=True,
    )
    fetched = rows_at(arrived, slot_flat)
    fetched = fetched.reshape(heads_here, blocks_here, RANDOM, BLOCK, 2, DH)
    holder_glob = global_blocks // blocks_here
    place_glob = global_blocks % blocks_here
    mine_glob = holder_glob == my_index
    global_q_local = blocks_at(query_block_tiles, place_glob)
    global_kv_local = blocks_at(own_tiles, place_glob)
    owned_mask = mine_glob.astype(jnp.float32)
    summed_query, summed_pairs = lax.psum(
        (
            global_q_local.astype(jnp.float32) * owned_mask[None, :, None, None],
            global_kv_local.astype(jnp.float32) * owned_mask[None, :, None, None, None],
        ),
        "seq",
    )
    global_query = summed_query.astype(jnp.bfloat16)
    global_pairs = summed_pairs.astype(jnp.bfloat16)
    window = jnp.stack([kv_tiles[:, :-2], kv_tiles[:, 1:-1], kv_tiles[:, 2:]], axis=2)
    spread_global = jnp.broadcast_to(
        global_pairs[:, None], (heads_here, blocks_here, GLOBAL, BLOCK, 2, DH)
    )
    listed = jnp.concatenate([window, fetched, spread_global], axis=2).reshape(
        heads_here, blocks_here, -1, 2, DH
    )
    window_key_rows = listed[:, :, :, 0]
    window_value_rows = listed[:, :, :, 1]
    logit_scores = (
        jnp.einsum(
            "hbqd,hbkd->hbqk",
            query_block_tiles,
            window_key_rows,
            preferred_element_type=jnp.float32,
        )
        * score_multiplier
    )
    column_block = jnp.arange(window_key_rows.shape[2]) // BLOCK
    row_global = my_index * blocks_here + jnp.arange(blocks_here)
    valid_keys = jnp.where(
        column_block[None, :] == 0,
        row_global[:, None] > 0,
        jnp.where(column_block[None, :] == 2, row_global[:, None] < shards * blocks_here - 1, True),
    )
    logit_scores = jnp.where(valid_keys[None, :, None, :], logit_scores, -jnp.inf)
    row_peak = jnp.max(logit_scores, axis=-1, keepdims=True)
    exponent = jnp.exp(logit_scores - row_peak)
    softmax_divisor = jnp.sum(exponent, axis=-1, keepdims=True)
    sparse_result = (
        jnp.einsum(
            "hbqk,hbkd->hbqd",
            exponent.astype(jnp.bfloat16),
            window_value_rows,
            preferred_element_type=jnp.float32,
        )
        / softmax_divisor
    )
    sparse_result = sparse_result.astype(jnp.bfloat16)
    local_keys = own_tiles[:, :, :, 0].reshape(heads_here, tok_rows, DH)
    local_values = own_tiles[:, :, :, 1].reshape(heads_here, tok_rows, DH).astype(jnp.float32)
    global_rows_q = global_query.reshape(heads_here, GLOBAL * BLOCK, DH)
    global_scores = (
        jnp.einsum("hqd,hkd->hqk", global_rows_q, local_keys, preferred_element_type=jnp.float32)
        * score_multiplier
    )
    local_top = jnp.max(global_scores, axis=-1)
    global_exp = jnp.exp(global_scores - local_top[..., None])
    top_all, total_all, out_all = joined(
        (
            local_top,
            jnp.sum(global_exp, axis=-1),
            jnp.einsum("hqk,hkd->hqd", global_exp, local_values, precision=lax.Precision.HIGHEST),
        ),
        "seq",
        combine_parts,
    )
    global_out = (
        (out_all / total_all[..., None]).astype(jnp.bfloat16).reshape(heads_here, GLOBAL, BLOCK, DH)
    )
    block_ids = jnp.arange(blocks_here)
    for glob_index in range(GLOBAL):
        replace_mask = mine_glob[glob_index] & (block_ids == place_glob[glob_index])
        sparse_result = jnp.where(
            replace_mask[None, :, None, None], global_out[:, glob_index][:, None], sparse_result
        )
    attention = sparse_result.transpose(1, 2, 0, 3).reshape(tok_rows, features)
    partial_out = jnp.dot(attention, out_weight, preferred_element_type=jnp.float32)
    return lax.psum_scatter(
        partial_out.astype(jnp.bfloat16), "heads", scatter_dimension=1, tiled=True
    )


MESH = pl.DeviceIdType.MESH
ANY = pl.BlockSpec(memory_space=pl.ANY)
VMEM_BYTES = 56 * 1024 * 1024
SIDE = 2
CORES = 2
TILE = 1024


PLAN = ((3, (0,), ()), (4, (1, 2), ()), (5, (3,), (0, 1)), (6, (), (2,)), (7, (), (3,)))


def peers(shards, groups, me, group):
    line = [{"seq": lax.rem(me + k, shards)} for k in range(1, shards)]
    return line + [{"heads": lax.rem(group + k, groups)} for k in range(1, groups)]


def remote(src, dst, send, recv, device):
    return pltpu.make_async_remote_copy(
        src_ref=src,
        dst_ref=dst,
        send_sem=send,
        recv_sem=recv,
        device_id=device,
        device_id_type=MESH,
    )


def crossed(a, b, shards):
    total, bit = 0, 1
    while bit < shards:
        if isinstance(b, int):
            here, there = lax.rem(lax.div(a, bit), 2), (b // bit) % 2
        else:
            here, there = lax.rem(lax.div(a, bit), 2), lax.rem(lax.div(b, bit), 2)
        total = total + bit * (here + there - 2 * here * there)
        bit *= 2
    return total


def layer_kernel(
    shards, heads, groups,
    q_ref, k_ref, v_ref, list_ref, glob_ref, w_ref, out_ref,
    q_here, named, named_near, chosen, glob_all, glob_q, q_all, k_all, v_all, list_all, list_here,
    w_here, glob_here, glob_peak, glob_total, o_here, att, acc,
    send_sem, recv_sem, pass_send, pass_recv, w_send, w_recv, own_sem, glob_send, glob_recv,
    o_send, o_recv, side_send, side_recv, half_send, half_recv,
):
    me = lax.axis_index("seq")
    group = lax.axis_index("heads")
    rows, width = out_ref.shape
    depth = w_ref.shape[0]
    share = CORES
    piece = rows // share
    blocks = rows // BLOCK
    local = blocks // share
    last = shards * blocks - 1
    scale = DH ** (-0.5)
    nt = (((1,), (1,)), ((), ()))
    my_head = lax.div(me, share)
    my_part = lax.rem(me, share)
    partner = my_head * share + (1 - my_part)
    pairs = ((k_ref, k_all), (v_ref, v_all))
    count = len(pairs)

    outer = 1 - lax.rem(my_head + lax.div(my_head, 2), 2)

    def due(t, swapped):
        if isinstance(t, int):
            return t if t < 2 * share else t + swapped * share * (1 - 2 * (t // share % 2))
        far = lax.div(t, 2 * share)
        return t + swapped * far * share * (1 - 2 * lax.rem(lax.div(t, share), 2))

    barrier = pltpu.get_barrier_semaphore()
    known = peers(shards, groups, me, group)
    for device in known:
        pl.semaphore_signal(barrier, inc=1, device_id=device, device_id_type=MESH)

    def window(src, head, part):
        return src.at[
            pl.ds(part * local, local), :, pl.ds(pl.multiple_of(head * DH, DH), DH)
        ]

    def landing(dst, source, part):
        return dst.at[pl.ds(source * blocks + part * local, local)]

    load_q = pltpu.make_async_copy(q_ref, q_here, own_sem.at[0])
    load_q.start()
    own_kv = [
        pltpu.make_async_copy(
            window(src, my_head, my_part), landing(dst, me, my_part), own_sem.at[1 + t]
        )
        for t, (src, dst) in enumerate(pairs)
    ]
    own_q = pltpu.make_async_copy(
        window(q_ref, my_head, my_part), q_all.at[me], own_sem.at[3]
    )
    own_list = pltpu.make_async_copy(list_ref, list_all.at[me], own_sem.at[4])
    own_w = pltpu.make_async_copy(
        w_ref.at[:, pl.ds(pl.multiple_of(group * width, width), width)],
        w_here.at[group],
        own_sem.at[5],
    )
    for copy in (*own_kv, own_q, own_list, own_w):
        copy.start()
    load_q.wait()
    for r in range(GLOBAL):
        picked = q_here[lax.rem(glob_ref[r], blocks)]
        for head in range(heads):
            named[r, head] = picked[:, head * DH : (head + 1) * DH]
    pl.semaphore_wait(barrier, len(known))

    swap = remote(
        named.at[1 - my_part], named_near, glob_send.at[0], glob_recv.at[0], {"seq": partner}
    )
    swap.start()
    sends = {}
    for x in range(1, shards):
        sends[x, count] = remote(
            list_ref,
            list_all.at[me],
            send_sem.at[x, count],
            recv_sem.at[x, count],
            {"seq": crossed(me, x, shards)},
        )
        sends[x, count].start()

    def offer(x):
        to = crossed(me, x, shards)
        head, part = lax.div(to, share), lax.rem(to, share)
        for t, (src, dst) in enumerate(pairs):
            sends[x, t] = remote(
                window(src, head, part),
                landing(dst, me, part),
                send_sem.at[x, t],
                recv_sem.at[x, t],
                {"seq": to},
            )
            sends[x, t].start()

    for x in (2, shards // 2):
        offer(x)
    swap.wait_recv()
    wanted = lax.div(glob_ref[my_part], blocks)
    for head in range(heads):
        apart = jnp.full((BLOCK, DH), wanted, jnp.int32) - jnp.full((BLOCK, DH), partner, jnp.int32)
        chosen[head] = jnp.where(apart == 0, named_near[head], named[my_part, head])
    own_glob = pltpu.make_async_copy(chosen.at[my_head], glob_all.at[my_head], own_sem.at[0])
    own_glob.start()
    globs = {}
    for n in range(1, heads):
        to = crossed(me, n * share, shards)
        globs[n] = remote(
            chosen.at[lax.div(to, share)],
            glob_all.at[my_head],
            glob_send.at[n],
            glob_recv.at[n],
            {"seq": to},
        )
        globs[n].start()
    for x in range(1, shards):
        if x not in (2, shards // 2):
            offer(x)

    def weight_rows(of, part):
        slab = depth // share
        return w_here.at[of, pl.ds(pl.multiple_of(part * slab, slab), slab), :]

    def query(x):
        to = crossed(me, x, shards)
        return remote(
            window(q_ref, lax.div(to, share), lax.rem(to, share)),
            q_all.at[me],
            send_sem.at[x, count + 1],
            recv_sem.at[x, count + 1],
            {"seq": to},
        )

    for x in range(1, share + share):
        query(x).start()

    @pl.when(outer == 0)
    def _():
        for x in range(2 * share, shards - 2):
            query(due(x, outer)).start()

    own_list.wait()
    for x in range(1, shards):
        sends[x, count].wait_recv()
    told = pltpu.make_async_copy(list_all, list_here, own_sem.at[4])
    told.start()
    own_glob.wait()
    for n in range(1, heads):
        globs[n].wait_recv()
    glob_q[my_part] = glob_all[lax.div(wanted, share)]
    glob_pass = remote(
        glob_q.at[my_part], glob_q.at[my_part], glob_send.at[heads], glob_recv.at[heads], {"seq": partner}
    )
    glob_pass.start()
    weights = {}
    for k in range(1, groups):
        to = lax.rem(group + k, groups)
        slab = depth // share
        weights[k] = remote(
            w_ref.at[
                pl.ds(pl.multiple_of(my_part * slab, slab), slab),
                pl.ds(pl.multiple_of(to * width, width), width),
            ],
            weight_rows(group, my_part),
            w_send.at[0, k],
            w_recv.at[0, k],
            {"heads": to},
        )
        weights[k].start()

    told.wait()
    glob_pass.wait_recv()

    def offered(x, t):
        src, dst = pairs[t]
        return remote(
            window(src, 0, 0),
            landing(dst, me, my_part),
            send_sem.at[x, t],
            recv_sem.at[x, t],
            {"seq": crossed(me, x, shards)},
        )

    def handed(x, t):
        region = landing(pairs[t][1], crossed(me, x, shards), my_part)
        return remote(region, region, pass_send.at[x, t], pass_recv.at[x, t], {"seq": partner})

    size = GLOBAL * BLOCK
    glob_peak[...] = jnp.full((size, 1), -jnp.inf, jnp.float32)
    glob_total[...] = jnp.zeros((size, 1), jnp.float32)
    glob_here[...] = jnp.zeros((size, DH), jnp.float32)

    def step(c):
        at = pl.ds(c * blocks, blocks)
        scores = lax.dot_general(
            glob_q[...].reshape(size, DH),
            k_all[at].reshape(rows, DH),
            nt,
            preferred_element_type=jnp.float32,
        ) * scale
        peak = glob_peak[...]
        top = jnp.maximum(peak, jnp.max(scores, axis=-1, keepdims=True))
        fade = jnp.exp(peak - top)
        heavy = jnp.exp(scores - top)
        glob_peak[...] = top
        glob_total[...] = glob_total[...] * fade + jnp.sum(heavy, axis=-1, keepdims=True)
        glob_here[...] = glob_here[...] * fade + jnp.dot(
            heavy.astype(jnp.bfloat16),
            v_all[at].reshape(rows, DH),
            preferred_element_type=jnp.float32,
        )

    @pl.loop(0, heads + 1)
    def _(m):
        @pl.when(m < heads)
        def _():
            for p in range(share):
                x = due(m * share + p, outer)
                for t in range(count):
                    if p == 0:
                        @pl.when(m == 0)
                        def _(t=t):
                            own_kv[t].wait()

                        @pl.when(m > 0)
                        def _(x=x, t=t):
                            offered(x, t).wait_recv()
                    else:
                        offered(x, t).wait_recv()
                    handed(x, t).start()

        @pl.when(m > 0)
        def _():
            for p in range(share):
                for t in range(count):
                    handed(due((m - 1) * share + p, outer), t).wait_recv()
            chip = crossed(my_head, lax.div(due((m - 1) * share, outer), share), heads)
            for p in range(share):
                step(chip * share + p)

    @pl.when(outer == 1)
    def _():
        for x in range(2 * share, shards - 2):
            query(due(x, outer)).start()

    glob_here[...] = glob_here[...] / glob_total[...]
    for k in range(1, groups):
        weights[k].wait_recv()
        of = lax.rem(group + groups - k, groups)
        weights[k, 1] = remote(
            weight_rows(of, my_part),
            weight_rows(of, my_part),
            w_send.at[1, k],
            w_recv.at[1, k],
            {"seq": partner},
        )
        weights[k, 1].start()
    own_q.wait()

    lanes = (3 + RANDOM + GLOBAL) * BLOCK
    column = lax.broadcasted_iota(jnp.int32, (1, lanes), 1) // BLOCK

    def one(i, s, j):
        here = my_part * local + j
        b = s * blocks + here
        listed = [jnp.maximum(b - 1, 0), b, jnp.minimum(b + 1, last)]
        for r in range(RANDOM):
            listed.append(list_here[s, r, my_head, here])
        for r in range(GLOBAL):
            listed.append(glob_ref[r])
        keys = jnp.concatenate([k_all[x] for x in listed], axis=0)
        values = jnp.concatenate([v_all[x] for x in listed], axis=0)
        scores = lax.dot_general(
            q_all[s, j], keys, nt, preferred_element_type=jnp.float32
        ) * scale
        hidden = ((column == 0) & (b == 0)) | ((column == 2) & (b == last))
        scores = jnp.where(hidden, -jnp.inf, scores)
        peak = jnp.max(scores, axis=-1, keepdims=True)
        heavy = jnp.exp(scores - peak)
        total = jnp.sum(heavy, axis=-1, keepdims=True)
        mixed = jnp.dot(heavy.astype(jnp.bfloat16), values, preferred_element_type=jnp.float32)
        result = mixed / total
        for r in range(GLOBAL):
            apart = jnp.full((BLOCK, DH), b, jnp.int32) - jnp.full((BLOCK, DH), glob_ref[r], jnp.int32)
            result = jnp.where(apart == 0, glob_here[r * BLOCK : (r + 1) * BLOCK, :], result)
        o_here[i, j * BLOCK : (j + 1) * BLOCK, :] = result.astype(jnp.bfloat16)

    across = lax.div(group, SIDE)
    along = lax.rem(group, SIDE)
    sides = (across * SIDE + (1 - along), (1 - across) * SIDE + along)
    diagonal = (1 - across) * SIDE + (1 - along)

    def spot(of, source):
        part = lax.rem(source, share)
        return att.at[
            of,
            pl.ds(pl.multiple_of(part * piece, piece), piece),
            pl.ds(pl.multiple_of(lax.div(source, share) * DH, DH), DH),
        ]

    def asked(i):
        return remote(
            window(q_ref, 0, 0),
            q_all.at[me],
            send_sem.at[i, count + 1],
            recv_sem.at[i, count + 1],
            {"seq": crossed(me, i, shards)},
        )

    def kept():
        return pltpu.make_async_copy(o_here.at[0], spot(group, me), own_sem.at[0])

    def back(i):
        return remote(
            o_here.at[i],
            spot(group, me),
            o_send.at[i],
            o_recv.at[i],
            {"seq": crossed(me, i, shards)},
        )

    def sideways(i, n):
        region = spot(group, crossed(me, i, shards))
        return remote(
            region, region, side_send.at[n, i], side_recv.at[n, i], {"heads": sides[n]}
        )

    def corner(i, n):
        half = piece // 2
        region = spot(sides[n], crossed(me, i, shards)).at[n * half : (n + 1) * half, :]
        return remote(
            region, region, half_send.at[n, i], half_recv.at[n, i], {"heads": sides[1 - n]}
        )

    def spread(i):
        if not isinstance(i, int):
            back(i).wait_recv()
        elif i == 0:
            kept().wait()
        else:
            back(i).wait_recv()
        for n in range(SIDE):
            sideways(i, n).start()

    def turn(i):
        for n in range(SIDE):
            sideways(i, n).wait_recv()
            corner(i, n).start()

    def arrive(i):
        for n in range(SIDE):
            corner(i, n).wait_recv()

    @pl.loop(0, shards)
    def _(n):
        i = due(n + share * (1 - 2 * lax.rem(lax.div(n, share), 2)) * (1 - lax.div(n, 2 * share)), outer)
        s = crossed(me, i, shards)

        @pl.when(i > 0)
        def _():
            asked(i).wait_recv()

        for j in range(local):
            one(i, s, j)

        @pl.when(i == 0)
        def _():
            kept().start()

        @pl.when(i > 0)
        def _():
            back(i).start()

        @pl.when(n == 1)
        def _():
            query(due(shards - 2, outer)).start()

        @pl.when(n == 3)
        def _():
            query(due(shards - 1, outer)).start()

        for when, spreads, turns in PLAN:
            @pl.when(n == when)
            def _(spreads=spreads, turns=turns):
                for at in spreads:
                    spread(at)
                for at in turns:
                    turn(at)

    half_depth = depth // 2
    my_side = lax.div(my_head, heads // 2)

    def project(parts, near, slices, first=False, final=False):
        base = (my_side if near else 1 - my_side) * half_depth
        deep = pl.ds(pl.multiple_of(base, half_depth), half_depth)

        for part in slices:
            at = pl.ds(pl.multiple_of(part * piece, piece), piece)

            @pl.loop(0, width // TILE)
            def _(c):
                cols = pl.ds(pl.multiple_of(c * TILE, TILE), TILE)
                term = sum(
                    jnp.dot(
                        att[of, at, deep],
                        w_here[of, deep, cols],
                        preferred_element_type=jnp.float32,
                    )
                    for of in parts
                )
                if not first:
                    term = term + acc[at, cols]
                if final:
                    out_ref[at, cols] = term.astype(out_ref.dtype)
                else:
                    acc[at, cols] = term

    def project_piece(i, parts, final=False):
        source = crossed(me, i, shards)
        at = pl.ds(pl.multiple_of(lax.rem(source, share) * piece, piece), piece)
        deep = pl.ds(pl.multiple_of(lax.div(source, share) * DH, DH), DH)

        @pl.loop(0, width // TILE)
        def _(c):
            cols = pl.ds(pl.multiple_of(c * TILE, TILE), TILE)
            term = acc[at, cols] + jnp.dot(
                jnp.concatenate([att[of, at, deep] for of in parts], axis=1),
                jnp.concatenate([w_here[of, deep, cols] for of in parts], axis=0),
                preferred_element_type=jnp.float32,
            )
            if final:
                out_ref[at, cols] = term.astype(out_ref.dtype)
            else:
                acc[at, cols] = term

    both = (my_part, 1 - my_part)
    ends = (group, diagonal)
    near_end = shards // 2
    own_w.wait()
    for k in range(1, groups):
        weights[k, 1].wait_recv()
    project((group,), True, both, first=True)
    spread(due(near_end, outer))

    @pl.when(outer == 1)
    def _():
        spread(due(near_end + 1, outer))
        turn(due(near_end, outer))

    for i in range(near_end):
        arrive(i)
    project((*sides, diagonal), True, both)

    @pl.when(outer == 0)
    def _():
        spread(due(near_end + 1, outer))
        turn(due(near_end, outer))

    for i in range(near_end + 2, shards):
        spread(due(i, outer))
        turn(due(i - 1, outer))
        arrive(due(i - 2, outer))
        project_piece(due(i - 2, outer), sides)
        project_piece(due(i - 2, outer), ends)
    turn(due(shards - 1, outer))
    arrive(due(shards - 2, outer))
    project_piece(due(shards - 2, outer), sides)
    project_piece(due(shards - 2, outer), ends, final=True)
    project_piece(due(shards - 1, outer), sides)
    arrive(due(shards - 1, outer))
    project_piece(due(shards - 1, outer), ends, final=True)

    swap.wait_send()
    glob_pass.wait_send()
    for copy in (*sends.values(), *globs.values(), *weights.values()):
        copy.wait_send()

    @pl.loop(0, shards)
    def _(i):
        for t in range(count):
            handed(i, t).wait_send()

        @pl.when(i > 0)
        def _():
            query(i).wait_send()
            back(i).wait_send()

        for n in range(SIDE):
            sideways(i, n).wait_send()
            corner(i, n).wait_send()


def regrouped(queries, key_vectors, value_vectors, random_blocks, global_blocks, out_weight):
    shards = lax.axis_size("seq")
    groups = lax.axis_size("heads")
    rows, features = queries.shape
    heads = features // DH
    blocks = rows // BLOCK
    piece = rows // CORES
    depth, model = out_weight.shape
    width = model // groups
    lists = random_blocks.transpose(2, 0, 1)
    dma = pltpu.SemaphoreType.DMA
    bf16 = jnp.bfloat16
    whole = pltpu.VMEM((shards * blocks, BLOCK, DH), bf16)
    split = (blocks, BLOCK, features)
    return pl.pallas_call(
        functools.partial(layer_kernel, shards, heads, groups),
        out_shape=pltpu.VMEM((rows, width), bf16),
        in_specs=[ANY] * 4 + [pl.BlockSpec(memory_space=pltpu.SMEM), ANY],
        out_specs=pl.BlockSpec(memory_space=pltpu.VMEM),
        scratch_shapes=[
            pltpu.VMEM(split, bf16),
            pltpu.VMEM((GLOBAL, heads, BLOCK, DH), bf16),
            pltpu.VMEM((heads, BLOCK, DH), bf16),
            pltpu.VMEM((heads, BLOCK, DH), bf16),
            pltpu.VMEM((heads, BLOCK, DH), bf16),
            pltpu.VMEM((GLOBAL, BLOCK, DH), bf16),
            pltpu.VMEM((shards, blocks // CORES, BLOCK, DH), bf16),
            whole,
            whole,
            pltpu.VMEM((shards, *lists.shape), jnp.int32),
            pltpu.SMEM((shards, *lists.shape), jnp.int32),
            pltpu.VMEM((groups, depth, width), bf16),
            pltpu.VMEM((GLOBAL * BLOCK, DH), jnp.float32),
            pltpu.VMEM((GLOBAL * BLOCK, 1), jnp.float32),
            pltpu.VMEM((GLOBAL * BLOCK, 1), jnp.float32),
            pltpu.VMEM((shards, piece, DH), bf16),
            pltpu.VMEM((groups, rows, features), bf16),
            pltpu.VMEM((rows, width), jnp.float32),
            dma((shards, 4)),
            dma((shards, 4)),
            dma((shards, 2)),
            dma((shards, 2)),
            dma((2, groups)),
            dma((2, groups)),
            dma((6,)),
            dma((heads + 1,)),
            dma((heads + 1,)),
            dma((shards,)),
            dma((shards,)),
            dma((SIDE, shards)),
            dma((SIDE, shards)),
            dma((SIDE, shards)),
            dma((SIDE, shards)),
        ],
        compiler_params=pltpu.CompilerParams(
            collective_id=0, has_side_effects=True, vmem_limit_bytes=VMEM_BYTES
        ),
        name="layer",
    )(
        queries.reshape(split),
        key_vectors.reshape(split),
        value_vectors.reshape(split),
        lists,
        global_blocks,
        out_weight,
    )


def on_device(queries, key_vectors, value_vectors, random_blocks, global_blocks, out_weight):
    shards = lax.axis_size("seq")
    groups = lax.axis_size("heads")
    rows, features = queries.shape
    heads = features // DH
    fits = shards == heads * CORES and heads == 4 and groups == SIDE * SIDE and GLOBAL == CORES
    fits = fits and (out_weight.shape[1] // groups) % TILE == 0
    body = regrouped if fits and (rows // BLOCK) % CORES == 0 else requested
    return body(queries, key_vectors, value_vectors, random_blocks, global_blocks, out_weight)


def solution(mesh):
    placed = (
        P("seq", "heads"),
        P("seq", "heads"),
        P("seq", "heads"),
        P("heads", "seq", None),
        P(),
        P("heads", None),
    )
    return jax.shard_map(
        on_device, mesh=mesh, in_specs=placed, out_specs=P("seq", "heads"), check_vma=False
    )
```

```python
import functools

import jax
import jax.numpy as jnp
from jax import lax
from jax.experimental import pallas as pl
from jax.experimental.pallas import tpu as pltpu
from jax.sharding import PartitionSpec as P

DH = 128
BLOCK = 64
RANDOM = 3
GLOBAL = 2


def extended(shard, sides, width):
    for axis, dim in sides:
        peers, length = (lax.axis_size(axis), shard.shape[dim])
        up = [(i, (i + 1) % peers) for i in range(peers - 1)]
        down = [(j, i) for i, j in up]
        last = lax.slice_in_dim(shard, length - width, length, axis=dim)
        leading = lax.slice_in_dim(shard, 0, width, axis=dim)
        before = lax.ppermute(last, axis, up)
        after = lax.ppermute(leading, axis, down)
        shard = jnp.concatenate([before, shard, after], axis=dim)
    return shard


def joined(shard, axis, combine):
    everything = jax.tree.map(
        lambda part, kind: lax.all_gather(part.astype(kind), axis),
        shard,
        (jnp.bfloat16, jnp.bfloat16, jnp.bfloat16),
    )

    def take(k):
        return jax.tree.map(lambda part, own: part[k].astype(own.dtype), everything, shard)

    return lax.fori_loop(
        1, lax.axis_size(axis), lambda k, so_far: combine(so_far, take(k)), take(0)
    )


def combine_parts(first, second):
    top_first, total_first, out_first = first
    top_second, total_second, out_second = second
    highest = jnp.maximum(top_first, top_second)
    scale_first = jnp.exp(top_first - highest)
    scale_second = jnp.exp(top_second - highest)
    return (
        highest,
        total_first * scale_first + total_second * scale_second,
        out_first * scale_first[..., None] + out_second * scale_second[..., None],
    )


def rows_at(table, index):
    chosen = (index[:, None] == jnp.arange(table.shape[0], dtype=jnp.int32)[None, :]).astype(table.dtype)
    return jnp.dot(chosen, table, preferred_element_type=jnp.float32).astype(table.dtype)


def blocks_at(tiles, index):
    return jnp.stack([lax.dynamic_index_in_dim(tiles, index[r], 1, False) for r in range(GLOBAL)], axis=1)


def requested(queries, key_vectors, value_vectors, random_blocks, global_blocks, out_weight):
    shards = lax.axis_size("seq")
    my_index = lax.axis_index("seq")
    tok_rows, features = queries.shape
    heads_here = features // DH
    blocks_here = tok_rows // BLOCK
    requests = heads_here * blocks_here * RANDOM
    capacity = max(2, 3 * requests // (2 * shards) + 1)
    score_multiplier = DH ** (-0.5)
    query_block_tiles = queries.reshape(blocks_here, BLOCK, heads_here, DH).transpose(2, 0, 1, 3)
    stacked = jnp.concatenate([key_vectors, value_vectors], axis=1)
    padded = extended(stacked, (("seq", 0),), BLOCK)
    kv_tiles = padded.reshape(blocks_here + 2, BLOCK, 2, heads_here, DH).transpose(3, 0, 1, 2, 4)
    own_tiles = kv_tiles[:, 1:-1]
    table = own_tiles.reshape(heads_here * blocks_here, BLOCK * 2 * DH)
    flat_lists = random_blocks.reshape(requests)
    head_of = jnp.arange(requests, dtype=jnp.int32) // (blocks_here * RANDOM)
    code_flat = head_of * blocks_here + flat_lists % blocks_here
    holders = flat_lists // blocks_here
    order = jnp.arange(requests, dtype=jnp.int32)
    earlier = (order[None, :] < order[:, None]) & (holders[None, :] == holders[:, None])
    slot_flat = holders * capacity + jnp.sum(earlier.astype(jnp.int32), axis=1)
    slots = jnp.arange(shards * capacity, dtype=jnp.int32)
    asked = jnp.sum(
        jnp.where(slots[:, None] == slot_flat[None, :], code_flat[None, :], 0), axis=1
    ).reshape(shards, capacity)
    answered = lax.all_to_all(asked, "seq", split_axis=0, concat_axis=0, tiled=True)
    arrived = lax.all_to_all(
        rows_at(table, answered.reshape(shards * capacity)),
        "seq",
        split_axis=0,
        concat_axis=0,
        tiled=True,
    )
    fetched = rows_at(arrived, slot_flat)
    fetched = fetched.reshape(heads_here, blocks_here, RANDOM, BLOCK, 2, DH)
    holder_glob = global_blocks // blocks_here
    place_glob = global_blocks % blocks_here
    mine_glob = holder_glob == my_index
    global_q_local = blocks_at(query_block_tiles, place_glob)
    global_kv_local = blocks_at(own_tiles, place_glob)
    owned_mask = mine_glob.astype(jnp.float32)
    summed_query, summed_pairs = lax.psum(
        (
            global_q_local.astype(jnp.float32) * owned_mask[None, :, None, None],
            global_kv_local.astype(jnp.float32) * owned_mask[None, :, None, None, None],
        ),
        "seq",
    )
    global_query = summed_query.astype(jnp.bfloat16)
    global_pairs = summed_pairs.astype(jnp.bfloat16)
    window = jnp.stack([kv_tiles[:, :-2], kv_tiles[:, 1:-1], kv_tiles[:, 2:]], axis=2)
    spread_global = jnp.broadcast_to(
        global_pairs[:, None], (heads_here, blocks_here, GLOBAL, BLOCK, 2, DH)
    )
    listed = jnp.concatenate([window, fetched, spread_global], axis=2).reshape(
        heads_here, blocks_here, -1, 2, DH
    )
    window_key_rows = listed[:, :, :, 0]
    window_value_rows = listed[:, :, :, 1]
    logit_scores = (
        jnp.einsum(
            "hbqd,hbkd->hbqk",
            query_block_tiles,
            window_key_rows,
            preferred_element_type=jnp.float32,
        )
        * score_multiplier
    )
    column_block = jnp.arange(window_key_rows.shape[2]) // BLOCK
    row_global = my_index * blocks_here + jnp.arange(blocks_here)
    valid_keys = jnp.where(
        column_block[None, :] == 0,
        row_global[:, None] > 0,
        jnp.where(column_block[None, :] == 2, row_global[:, None] < shards * blocks_here - 1, True),
    )
    logit_scores = jnp.where(valid_keys[None, :, None, :], logit_scores, -jnp.inf)
    row_peak = jnp.max(logit_scores, axis=-1, keepdims=True)
    exponent = jnp.exp(logit_scores - row_peak)
    softmax_divisor = jnp.sum(exponent, axis=-1, keepdims=True)
    sparse_result = (
        jnp.einsum(
            "hbqk,hbkd->hbqd",
            exponent.astype(jnp.bfloat16),
            window_value_rows,
            preferred_element_type=jnp.float32,
        )
        / softmax_divisor
    )
    sparse_result = sparse_result.astype(jnp.bfloat16)
    local_keys = own_tiles[:, :, :, 0].reshape(heads_here, tok_rows, DH)
    local_values = own_tiles[:, :, :, 1].reshape(heads_here, tok_rows, DH).astype(jnp.float32)
    global_rows_q = global_query.reshape(heads_here, GLOBAL * BLOCK, DH)
    global_scores = (
        jnp.einsum("hqd,hkd->hqk", global_rows_q, local_keys, preferred_element_type=jnp.float32)
        * score_multiplier
    )
    local_top = jnp.max(global_scores, axis=-1)
    global_exp = jnp.exp(global_scores - local_top[..., None])
    top_all, total_all, out_all = joined(
        (
            local_top,
            jnp.sum(global_exp, axis=-1),
            jnp.einsum("hqk,hkd->hqd", global_exp, local_values, precision=lax.Precision.HIGHEST),
        ),
        "seq",
        combine_parts,
    )
    global_out = (
        (out_all / total_all[..., None]).astype(jnp.bfloat16).reshape(heads_here, GLOBAL, BLOCK, DH)
    )
    block_ids = jnp.arange(blocks_here)
    for glob_index in range(GLOBAL):
        replace_mask = mine_glob[glob_index] & (block_ids == place_glob[glob_index])
        sparse_result = jnp.where(
            replace_mask[None, :, None, None], global_out[:, glob_index][:, None], sparse_result
        )
    attention = sparse_result.transpose(1, 2, 0, 3).reshape(tok_rows, features)
    partial_out = jnp.dot(attention, out_weight, preferred_element_type=jnp.float32)
    return lax.psum_scatter(
        partial_out.astype(jnp.bfloat16), "heads", scatter_dimension=1, tiled=True
    )


MESH = pl.DeviceIdType.MESH
ANY = pl.BlockSpec(memory_space=pl.ANY)
VMEM_BYTES = 56 * 1024 * 1024
SIDE = 2
CORES = 2
TILE = 1024


PLAN = ((3, (0,), ()), (4, (1, 2), ()), (5, (3,), (0, 1)), (6, (), (2,)), (7, (), (3,)))


def peers(shards, groups, me, group):
    line = [{"seq": lax.rem(me + k, shards)} for k in range(1, shards)]
    return line + [{"heads": lax.rem(group + k, groups)} for k in range(1, groups)]


def remote(src, dst, send, recv, device):
    return pltpu.make_async_remote_copy(
        src_ref=src,
        dst_ref=dst,
        send_sem=send,
        recv_sem=recv,
        device_id=device,
        device_id_type=MESH,
    )


def crossed(a, b, shards):
    total, bit = 0, 1
    while bit < shards:
        if isinstance(b, int):
            here, there = lax.rem(lax.div(a, bit), 2), (b // bit) % 2
        else:
            here, there = lax.rem(lax.div(a, bit), 2), lax.rem(lax.div(b, bit), 2)
        total = total + bit * (here + there - 2 * here * there)
        bit *= 2
    return total


def layer_kernel(
    shards, heads, groups,
    q_ref, k_ref, v_ref, list_ref, glob_ref, w_ref, out_ref,
    q_here, named, named_near, chosen, glob_all, glob_q, q_all, k_all, v_all, list_all, list_here,
    w_here, glob_here, glob_peak, glob_total, o_here, att, acc,
    send_sem, recv_sem, pass_send, pass_recv, w_send, w_recv, own_sem, glob_send, glob_recv,
    o_send, o_recv, side_send, side_recv, half_send, half_recv,
):
    me = lax.axis_index("seq")
    group = lax.axis_index("heads")
    rows, width = out_ref.shape
    depth = w_ref.shape[0]
    share = CORES
    piece = rows // share
    blocks = rows // BLOCK
    local = blocks // share
    last = shards * blocks - 1
    scale = DH ** (-0.5)
    nt = (((1,), (1,)), ((), ()))
    my_head = lax.div(me, share)
    my_part = lax.rem(me, share)
    partner = my_head * share + (1 - my_part)
    pairs = ((k_ref, k_all), (v_ref, v_all))
    count = len(pairs)

    outer = 1 - lax.rem(my_head + lax.div(my_head, 2), 2)

    def due(t, swapped):
        if isinstance(t, int):
            return t if t < 2 * share else t + swapped * share * (1 - 2 * (t // share % 2))
        far = lax.div(t, 2 * share)
        return t + swapped * far * share * (1 - 2 * lax.rem(lax.div(t, share), 2))

    barrier = pltpu.get_barrier_semaphore()
    known = peers(shards, groups, me, group)
    for device in known:
        pl.semaphore_signal(barrier, inc=1, device_id=device, device_id_type=MESH)

    def window(src, head, part):
        return src.at[
            pl.ds(part * local, local), :, pl.ds(pl.multiple_of(head * DH, DH), DH)
        ]

    def landing(dst, source, part):
        return dst.at[pl.ds(source * blocks + part * local, local)]

    load_q = pltpu.make_async_copy(q_ref, q_here, own_sem.at[0])
    load_q.start()
    own_kv = [
        pltpu.make_async_copy(
            window(src, my_head, my_part), landing(dst, me, my_part), own_sem.at[1 + t]
        )
        for t, (src, dst) in enumerate(pairs)
    ]
    own_q = pltpu.make_async_copy(
        window(q_ref, my_head, my_part), q_all.at[me], own_sem.at[3]
    )
    own_list = pltpu.make_async_copy(list_ref, list_all.at[me], own_sem.at[4])
    own_w = pltpu.make_async_copy(
        w_ref.at[:, pl.ds(pl.multiple_of(group * width, width), width)],
        w_here.at[group],
        own_sem.at[5],
    )
    for copy in (*own_kv, own_q, own_list, own_w):
        copy.start()
    load_q.wait()
    for r in range(GLOBAL):
        picked = q_here[lax.rem(glob_ref[r], blocks)]
        for head in range(heads):
            named[r, head] = picked[:, head * DH : (head + 1) * DH]
    pl.semaphore_wait(barrier, len(known))

    swap = remote(
        named.at[1 - my_part], named_near, glob_send.at[0], glob_recv.at[0], {"seq": partner}
    )
    swap.start()
    sends = {}
    for x in range(1, shards):
        sends[x, count] = remote(
            list_ref,
            list_all.at[me],
            send_sem.at[x, count],
            recv_sem.at[x, count],
            {"seq": crossed(me, x, shards)},
        )
        sends[x, count].start()

    def offer(x):
        to = crossed(me, x, shards)
        head, part = lax.div(to, share), lax.rem(to, share)
        for t, (src, dst) in enumerate(pairs):
            sends[x, t] = remote(
                window(src, head, part),
                landing(dst, me, part),
                send_sem.at[x, t],
                recv_sem.at[x, t],
                {"seq": to},
            )
            sends[x, t].start()

    for x in (2, shards // 2):
        offer(x)
    swap.wait_recv()
    wanted = lax.div(glob_ref[my_part], blocks)
    for head in range(heads):
        apart = jnp.full((BLOCK, DH), wanted, jnp.int32) - jnp.full((BLOCK, DH), partner, jnp.int32)
        chosen[head] = jnp.where(apart == 0, named_near[head], named[my_part, head])
    own_glob = pltpu.make_async_copy(chosen.at[my_head], glob_all.at[my_head], own_sem.at[0])
    own_glob.start()
    globs = {}
    for n in range(1, heads):
        to = crossed(me, n * share, shards)
        globs[n] = remote(
            chosen.at[lax.div(to, share)],
            glob_all.at[my_head],
            glob_send.at[n],
            glob_recv.at[n],
            {"seq": to},
        )
        globs[n].start()
    for x in range(1, shards):
        if x not in (2, shards // 2):
            offer(x)

    def weight_rows(of, part):
        slab = depth // share
        return w_here.at[of, pl.ds(pl.multiple_of(part * slab, slab), slab), :]

    def query(x):
        to = crossed(me, x, shards)
        return remote(
            window(q_ref, lax.div(to, share), lax.rem(to, share)),
            q_all.at[me],
            send_sem.at[x, count + 1],
            recv_sem.at[x, count + 1],
            {"seq": to},
        )

    for x in range(1, share + share):
        query(x).start()

    @pl.when(outer == 0)
    def _():
        for x in range(2 * share, shards - 2):
            query(due(x, outer)).start()

    own_list.wait()
    for x in range(1, shards):
        sends[x, count].wait_recv()
    told = pltpu.make_async_copy(list_all, list_here, own_sem.at[4])
    told.start()
    own_glob.wait()
    for n in range(1, heads):
        globs[n].wait_recv()
    glob_q[my_part] = glob_all[lax.div(wanted, share)]
    glob_pass = remote(
        glob_q.at[my_part], glob_q.at[my_part], glob_send.at[heads], glob_recv.at[heads], {"seq": partner}
    )
    glob_pass.start()
    weights = {}
    for k in range(1, groups):
        to = lax.rem(group + k, groups)
        slab = depth // share
        weights[k] = remote(
            w_ref.at[
                pl.ds(pl.multiple_of(my_part * slab, slab), slab),
                pl.ds(pl.multiple_of(to * width, width), width),
            ],
            weight_rows(group, my_part),
            w_send.at[0, k],
            w_recv.at[0, k],
            {"heads": to},
        )
        weights[k].start()

    told.wait()
    glob_pass.wait_recv()

    def offered(x, t):
        src, dst = pairs[t]
        return remote(
            window(src, 0, 0),
            landing(dst, me, my_part),
            send_sem.at[x, t],
            recv_sem.at[x, t],
            {"seq": crossed(me, x, shards)},
        )

    def handed(x, t):
        region = landing(pairs[t][1], crossed(me, x, shards), my_part)
        return remote(region, region, pass_send.at[x, t], pass_recv.at[x, t], {"seq": partner})

    size = GLOBAL * BLOCK
    glob_peak[...] = jnp.full((size, 1), -jnp.inf, jnp.float32)
    glob_total[...] = jnp.zeros((size, 1), jnp.float32)
    glob_here[...] = jnp.zeros((size, DH), jnp.float32)

    def step(c):
        at = pl.ds(c * blocks, blocks)
        scores = lax.dot_general(
            glob_q[...].reshape(size, DH),
            k_all[at].reshape(rows, DH),
            nt,
            preferred_element_type=jnp.float32,
        ) * scale
        peak = glob_peak[...]
        top = jnp.maximum(peak, jnp.max(scores, axis=-1, keepdims=True))
        fade = jnp.exp(peak - top)
        heavy = jnp.exp(scores - top)
        glob_peak[...] = top
        glob_total[...] = glob_total[...] * fade + jnp.sum(heavy, axis=-1, keepdims=True)
        glob_here[...] = glob_here[...] * fade + jnp.dot(
            heavy.astype(jnp.bfloat16),
            v_all[at].reshape(rows, DH),
            preferred_element_type=jnp.float32,
        )

    @pl.loop(0, heads + 1)
    def _(m):
        @pl.when(m < heads)
        def _():
            for p in range(share):
                x = due(m * share + p, outer)
                for t in range(count):
                    if p == 0:
                        @pl.when(m == 0)
                        def _(t=t):
                            own_kv[t].wait()

                        @pl.when(m > 0)
                        def _(x=x, t=t):
                            offered(x, t).wait_recv()
                    else:
                        offered(x, t).wait_recv()
                    handed(x, t).start()

        @pl.when(m > 0)
        def _():
            for p in range(share):
                for t in range(count):
                    handed(due((m - 1) * share + p, outer), t).wait_recv()
            chip = crossed(my_head, lax.div(due((m - 1) * share, outer), share), heads)
            for p in range(share):
                step(chip * share + p)

    @pl.when(outer == 1)
    def _():
        for x in range(2 * share, shards - 2):
            query(due(x, outer)).start()

    glob_here[...] = glob_here[...] / glob_total[...]
    for k in range(1, groups):
        weights[k].wait_recv()
        of = lax.rem(group + groups - k, groups)
        weights[k, 1] = remote(
            weight_rows(of, my_part),
            weight_rows(of, my_part),
            w_send.at[1, k],
            w_recv.at[1, k],
            {"seq": partner},
        )
        weights[k, 1].start()
    own_q.wait()

    lanes = (3 + RANDOM + GLOBAL) * BLOCK
    column = lax.broadcasted_iota(jnp.int32, (1, lanes), 1) // BLOCK

    def one(i, s, j):
        here = my_part * local + j
        b = s * blocks + here
        listed = [jnp.maximum(b - 1, 0), b, jnp.minimum(b + 1, last)]
        for r in range(RANDOM):
            listed.append(list_here[s, r, my_head, here])
        for r in range(GLOBAL):
            listed.append(glob_ref[r])
        keys = jnp.concatenate([k_all[x] for x in listed], axis=0)
        values = jnp.concatenate([v_all[x] for x in listed], axis=0)
        scores = lax.dot_general(
            q_all[s, j], keys, nt, preferred_element_type=jnp.float32
        ) * scale
        hidden = ((column == 0) & (b == 0)) | ((column == 2) & (b == last))
        scores = jnp.where(hidden, -jnp.inf, scores)
        peak = jnp.max(scores, axis=-1, keepdims=True)
        heavy = jnp.exp(scores - peak)
        total = jnp.sum(heavy, axis=-1, keepdims=True)
        mixed = jnp.dot(heavy.astype(jnp.bfloat16), values, preferred_element_type=jnp.float32)
        result = mixed / total
        for r in range(GLOBAL):
            apart = jnp.full((BLOCK, DH), b, jnp.int32) - jnp.full((BLOCK, DH), glob_ref[r], jnp.int32)
            result = jnp.where(apart == 0, glob_here[r * BLOCK : (r + 1) * BLOCK, :], result)
        o_here[i, j * BLOCK : (j + 1) * BLOCK, :] = result.astype(jnp.bfloat16)

    across = lax.div(group, SIDE)
    along = lax.rem(group, SIDE)
    sides = (across * SIDE + (1 - along), (1 - across) * SIDE + along)
    diagonal = (1 - across) * SIDE + (1 - along)

    def spot(of, source):
        part = lax.rem(source, share)
        return att.at[
            of,
            pl.ds(pl.multiple_of(part * piece, piece), piece),
            pl.ds(pl.multiple_of(lax.div(source, share) * DH, DH), DH),
        ]

    def asked(i):
        return remote(
            window(q_ref, 0, 0),
            q_all.at[me],
            send_sem.at[i, count + 1],
            recv_sem.at[i, count + 1],
            {"seq": crossed(me, i, shards)},
        )

    def kept():
        return pltpu.make_async_copy(o_here.at[0], spot(group, me), own_sem.at[0])

    def back(i):
        return remote(
            o_here.at[i],
            spot(group, me),
            o_send.at[i],
            o_recv.at[i],
            {"seq": crossed(me, i, shards)},
        )

    def sideways(i, n):
        region = spot(group, crossed(me, i, shards))
        return remote(
            region, region, side_send.at[n, i], side_recv.at[n, i], {"heads": sides[n]}
        )

    def corner(i, n):
        half = piece // 2
        region = spot(sides[n], crossed(me, i, shards)).at[n * half : (n + 1) * half, :]
        return remote(
            region, region, half_send.at[n, i], half_recv.at[n, i], {"heads": sides[1 - n]}
        )

    def spread(i):
        if not isinstance(i, int):
            back(i).wait_recv()
        elif i == 0:
            kept().wait()
        else:
            back(i).wait_recv()
        for n in range(SIDE):
            sideways(i, n).start()

    def turn(i):
        for n in range(SIDE):
            sideways(i, n).wait_recv()
            corner(i, n).start()

    def arrive(i):
        for n in range(SIDE):
            corner(i, n).wait_recv()

    @pl.loop(0, shards)
    def _(n):
        i = due(n + share * (1 - 2 * lax.rem(lax.div(n, share), 2)) * (1 - lax.div(n, 2 * share)), outer)
        s = crossed(me, i, shards)

        @pl.when(i > 0)
        def _():
            asked(i).wait_recv()

        for j in range(local):
            one(i, s, j)

        @pl.when(i == 0)
        def _():
            kept().start()

        @pl.when(i > 0)
        def _():
            back(i).start()

        @pl.when(n == 1)
        def _():
            query(due(shards - 2, outer)).start()

        @pl.when(n == 3)
        def _():
            query(due(shards - 1, outer)).start()

        for when, spreads, turns in PLAN:
            @pl.when(n == when)
            def _(spreads=spreads, turns=turns):
                for at in spreads:
                    spread(at)
                for at in turns:
                    turn(at)

    half_depth = depth // 2
    my_side = lax.div(my_head, heads // 2)

    def project(parts, near, slices, first=False, final=False):
        base = (my_side if near else 1 - my_side) * half_depth
        deep = pl.ds(pl.multiple_of(base, half_depth), half_depth)

        for part in slices:
            at = pl.ds(pl.multiple_of(part * piece, piece), piece)

            @pl.loop(0, width // TILE)
            def _(c):
                cols = pl.ds(pl.multiple_of(c * TILE, TILE), TILE)
                term = sum(
                    jnp.dot(
                        att[of, at, deep],
                        w_here[of, deep, cols],
                        preferred_element_type=jnp.float32,
                    )
                    for of in parts
                )
                if not first:
                    term = term + acc[at, cols]
                if final:
                    out_ref[at, cols] = term.astype(out_ref.dtype)
                else:
                    acc[at, cols] = term

    def project_piece(i, parts, final=False):
        source = crossed(me, i, shards)
        at = pl.ds(pl.multiple_of(lax.rem(source, share) * piece, piece), piece)
        deep = pl.ds(pl.multiple_of(lax.div(source, share) * DH, DH), DH)

        @pl.loop(0, width // TILE)
        def _(c):
            cols = pl.ds(pl.multiple_of(c * TILE, TILE), TILE)
            term = acc[at, cols] + jnp.dot(
                jnp.concatenate([att[of, at, deep] for of in parts], axis=1),
                jnp.concatenate([w_here[of, deep, cols] for of in parts], axis=0),
                preferred_element_type=jnp.float32,
            )
            if final:
                out_ref[at, cols] = term.astype(out_ref.dtype)
            else:
                acc[at, cols] = term

    both = (my_part, 1 - my_part)
    ends = (group, diagonal)
    near_end = shards // 2
    own_w.wait()
    for k in range(1, groups):
        weights[k, 1].wait_recv()
    project((group,), True, both, first=True)
    spread(due(near_end, outer))

    spread(due(near_end + 1, outer))
    turn(due(near_end, outer))

    for i in range(near_end):
        arrive(i)
    project((*sides, diagonal), True, both)

    for i in range(near_end + 2, shards):
        spread(due(i, outer))
        turn(due(i - 1, outer))
        arrive(due(i - 2, outer))
        project_piece(due(i - 2, outer), sides)
        project_piece(due(i - 2, outer), ends)
    turn(due(shards - 1, outer))
    arrive(due(shards - 2, outer))
    project_piece(due(shards - 2, outer), sides)
    project_piece(due(shards - 2, outer), ends, final=True)
    project_piece(due(shards - 1, outer), sides)
    arrive(due(shards - 1, outer))
    project_piece(due(shards - 1, outer), ends, final=True)

    swap.wait_send()
    glob_pass.wait_send()
    for copy in (*sends.values(), *globs.values(), *weights.values()):
        copy.wait_send()

    @pl.loop(0, shards)
    def _(i):
        for t in range(count):
            handed(i, t).wait_send()

        @pl.when(i > 0)
        def _():
            query(i).wait_send()
            back(i).wait_send()

        for n in range(SIDE):
            sideways(i, n).wait_send()
            corner(i, n).wait_send()


def regrouped(queries, key_vectors, value_vectors, random_blocks, global_blocks, out_weight):
    shards = lax.axis_size("seq")
    groups = lax.axis_size("heads")
    rows, features = queries.shape
    heads = features // DH
    blocks = rows // BLOCK
    piece = rows // CORES
    depth, model = out_weight.shape
    width = model // groups
    lists = random_blocks.transpose(2, 0, 1)
    dma = pltpu.SemaphoreType.DMA
    bf16 = jnp.bfloat16
    whole = pltpu.VMEM((shards * blocks, BLOCK, DH), bf16)
    split = (blocks, BLOCK, features)
    return pl.pallas_call(
        functools.partial(layer_kernel, shards, heads, groups),
        out_shape=pltpu.VMEM((rows, width), bf16),
        in_specs=[ANY] * 4 + [pl.BlockSpec(memory_space=pltpu.SMEM), ANY],
        out_specs=pl.BlockSpec(memory_space=pltpu.VMEM),
        scratch_shapes=[
            pltpu.VMEM(split, bf16),
            pltpu.VMEM((GLOBAL, heads, BLOCK, DH), bf16),
            pltpu.VMEM((heads, BLOCK, DH), bf16),
            pltpu.VMEM((heads, BLOCK, DH), bf16),
            pltpu.VMEM((heads, BLOCK, DH), bf16),
            pltpu.VMEM((GLOBAL, BLOCK, DH), bf16),
            pltpu.VMEM((shards, blocks // CORES, BLOCK, DH), bf16),
            whole,
            whole,
            pltpu.VMEM((shards, *lists.shape), jnp.int32),
            pltpu.SMEM((shards, *lists.shape), jnp.int32),
            pltpu.VMEM((groups, depth, width), bf16),
            pltpu.VMEM((GLOBAL * BLOCK, DH), jnp.float32),
            pltpu.VMEM((GLOBAL * BLOCK, 1), jnp.float32),
            pltpu.VMEM((GLOBAL * BLOCK, 1), jnp.float32),
            pltpu.VMEM((shards, piece, DH), bf16),
            pltpu.VMEM((groups, rows, features), bf16),
            pltpu.VMEM((rows, width), jnp.float32),
            dma((shards, 4)),
            dma((shards, 4)),
            dma((shards, 2)),
            dma((shards, 2)),
            dma((2, groups)),
            dma((2, groups)),
            dma((6,)),
            dma((heads + 1,)),
            dma((heads + 1,)),
            dma((shards,)),
            dma((shards,)),
            dma((SIDE, shards)),
            dma((SIDE, shards)),
            dma((SIDE, shards)),
            dma((SIDE, shards)),
        ],
        compiler_params=pltpu.CompilerParams(
            collective_id=0, has_side_effects=True, vmem_limit_bytes=VMEM_BYTES
        ),
        name="layer",
    )(
        queries.reshape(split),
        key_vectors.reshape(split),
        value_vectors.reshape(split),
        lists,
        global_blocks,
        out_weight,
    )


def on_device(queries, key_vectors, value_vectors, random_blocks, global_blocks, out_weight):
    shards = lax.axis_size("seq")
    groups = lax.axis_size("heads")
    rows, features = queries.shape
    heads = features // DH
    fits = shards == heads * CORES and heads == 4 and groups == SIDE * SIDE and GLOBAL == CORES
    fits = fits and (out_weight.shape[1] // groups) % TILE == 0
    body = regrouped if fits and (rows // BLOCK) % CORES == 0 else requested
    return body(queries, key_vectors, value_vectors, random_blocks, global_blocks, out_weight)


def solution(mesh):
    placed = (
        P("seq", "heads"),
        P("seq", "heads"),
        P("seq", "heads"),
        P("heads", "seq", None),
        P(),
        P("heads", None),
    )
    return jax.shard_map(
        on_device, mesh=mesh, in_specs=placed, out_specs=P("seq", "heads"), check_vma=False
    )
```
